32 devices in a mesh: ha: 2 (over core), wa: 4 (over y, x), ba: 4 (over z).
Axes of the slice: x: 2, y: 2, z: 4, core: 2. Of those that a mesh axis runs over, the one named last changes fastest.
Arguments:
- images: bfloat16 [168, 24, 24, 384], P('ba', 'ha', 'wa'), may hold values from -6 to 6
- out_grad: bfloat16 [168, 24, 24, 384], P('ba', 'ha', 'wa'), may hold values from -6 to 6
- keep_mask: int32 [168], P('ba'), may hold values 0 or 1
- img_counts: int32 [4], P('ba'), may hold values from 1 to 42, 87 in all
- mats_master: float32 [2, 384, 1536], P(None, None, 'ba'), may hold values from -0.3125 to 0.3125
- chan_master: float32 [54, 384], P(None, 'ba')
- bias_master: float32 [1536], P('ba'), may hold values from -3 to 3
- mats_moment: float32 [2, 384, 1536], P(None, None, 'ba'), may hold values from -1024 to 1024
- chan_moment: float32 [54, 384], P(None, 'ba'), may hold values from -1024 to 1024
- bias_moment: float32 [1536], P('ba'), may hold values from -1024 to 1024
- mats_second: float32 [2, 384, 1536], P(None, None, 'ba'), may hold values from 34836.48 to 139345.92
- chan_second: float32 [54, 384], P(None, 'ba'), may hold values from 34836.48 to 139345.92
- bias_second: float32 [1536], P('ba'), may hold values from 34836.48 to 139345.92
- mats_average: float32 [2, 384, 1536], P(None, None, 'ba'), may hold values from -0.3125 to 0.3125
- chan_average: float32 [54, 384], P(None, 'ba')
- bias_average: float32 [1536], P('ba'), may hold values from -3 to 3
Outputs:
- outputs: bfloat16 [168, 24, 24, 384], P('ba', 'ha', 'wa')
- input_grad: bfloat16 [168, 24, 24, 384], P('ba', 'ha', 'wa')
- mats_grad: float32 [2, 384, 1536], P(None, None, 'ba')
- chan_grad: float32 [54, 384], P(None, 'ba')
- bias_grad: float32 [1536], P('ba')
- mats_new: float32 [2, 384, 1536], P(None, None, 'ba')
- chan_new: float32 [54, 384], P(None, 'ba')
- bias_new: float32 [1536], P('ba')
- mats_moment_new: float32 [2, 384, 1536], P(None, None, 'ba')
- chan_moment_new: float32 [54, 384], P(None, 'ba')
- bias_moment_new: float32 [1536], P('ba')
- mats_second_new: float32 [2, 384, 1536], P(None, None, 'ba')
- chan_second_new: float32 [54, 384], P(None, 'ba')
- bias_second_new: float32 [1536], P('ba')
- mats_average_new: float32 [2, 384, 1536], P(None, None, 'ba')
- chan_average_new: float32 [54, 384], P(None, 'ba')
- bias_average_new: float32 [1536], P('ba')
- mats_low: bfloat16 [2, 384, 1536], P(None, None, 'ba')
- chan_low: bfloat16 [54, 384], P(None, 'ba')
- bias_low: bfloat16 [1536], P('ba')
The draws below stay inside these ranges and needn't reach their ends.
Inputs may be any that keep to these rules, and one draw needn't show every extreme that they name: `img_counts`: one index of ba holds exactly 42 filled slots.
All inputs are finite; a program needn't handle non-finite values. No bound on the sum of `keep_mask` or of `img_counts` on one device may be relied on, other than what follows from the above.
Results may differ from the reference program's by a relative error of at most 0.0098.
Values may be sent and summed in bfloat16 or wider, within the bound.
A program may use at most 192 MiB of HBM per device.

```python
import math
import jax
import jax.numpy as jnp
import numpy as np
from jax import lax

C = 384
HID = 1536
KS = 7
SIDE = 24
IMG_DEV = 42
STEP = 3
IMAGES = 168
NCH = 54
N_BA = 4


def channel_rows(key):
    keys = jax.random.split(key, 6)
    taps = jax.random.normal(keys[0], (KS * KS, C), jnp.float32) / KS
    conv_bias = 0.3 * jax.random.normal(keys[1], (1, C), jnp.float32)
    gain = jax.random.uniform(keys[2], (1, C), jnp.float32, 0.5, 1.5)
    shift = 0.3 * jax.random.normal(keys[3], (1, C), jnp.float32)
    out_bias = 0.3 * jax.random.normal(keys[4], (1, C), jnp.float32)
    scale = jnp.exp(jax.random.uniform(keys[5], (1, C), jnp.float32, -0.6931, 0.6931))
    return jnp.concatenate([taps, conv_bias, gain, shift, out_bias, scale], axis=0).astype(jnp.float32)


def draw_chan_master(key, part):
    return channel_rows(jax.random.fold_in(key, 11))


def draw_chan_average(key, part):
    return channel_rows(jax.random.fold_in(key, 12))


def plant(drawn, stream_key, least, largest):
    extent = drawn.shape
    index_at = [jax.random.randint(jax.random.fold_in(stream_key, axis), (), 0, extent[axis]) for axis in range(len(extent))]
    drawn = drawn.at[tuple(index_at)].set(least)
    longest = extent.index(max(extent))
    index_at[longest] = (index_at[longest] + 1) % extent[longest]
    return drawn.at[tuple(index_at)].set(largest)


def level_of(rng, extent, pieces, smallest, largest):
    def one(dim, blocks):
        draws = jax.random.uniform(jax.random.fold_in(jax.random.fold_in(rng, 6), dim), (blocks,), jnp.float32, smallest / len(pieces), largest / len(pieces))
        return jnp.repeat(jnp.exp(draws), extent[dim] // blocks).reshape((-1,) + (1,) * (len(extent) - dim - 1))

    level = one(*pieces[0])
    for cut in pieces[1:]:
        level = level * one(*cut)
    return level


def length_profile(number_of, total, most, skew):
    loads = [(1 << 20) // math.isqrt(standing ** skew) + 1 for standing in range(2, number_of + 1)]
    surplus, counts = total - most - (number_of - 1), [1] * (number_of - 1)
    while surplus > 0:
        movable = [i for i in range(number_of - 1) if counts[i] < most]
        pool, left = sum([loads[i] for i in movable]), surplus
        for i in movable:
            extra = min(most - counts[i], max(1, left * loads[i] // pool), surplus)
            counts[i] = counts[i] + extra
            surplus = surplus - extra
    return np.array([most] + counts)


def ragged_sizes(key, count, total, most, lean):
    if count == 2:
        one = jax.random.randint(key, (), max(1, total - most), min(most, total - 1) + 1)
        return jnp.stack([one, total - one])
    lengths = jnp.asarray(length_profile(count, total, most, lean), jnp.int32)
    pairs = (count - 1) // 2
    donor, sink = lengths[1:1 + 2 * pairs:2], lengths[2:2 + 2 * pairs:2]
    slack = jnp.minimum(donor - 1, most - sink)
    passed = jax.random.randint(jax.random.fold_in(key, 1), (pairs,), 0, 1 << 20) % (slack + 1)
    lengths = lengths.at[1:1 + 2 * pairs:2].set(donor - passed).at[2:2 + 2 * pairs:2].set(sink + passed)
    return lengths[jax.random.permutation(jax.random.fold_in(key, 2), count)]


def scatter_about(own_key, shape, scale, limit, cuts=(), kind=jnp.bfloat16):
    array = scale * jax.random.normal(own_key, shape, jnp.float32)
    if cuts:
        array = array * level_of(own_key, shape, cuts, -0.22, 0.18)
    return jnp.clip(array, -limit, limit).astype(kind)


def setup_inputs(seed: int = 0) -> dict:
    seeds = jax.random.split(jax.random.key(seed), 17)
    return {
        "images": scatter_about(seeds[0], (IMAGES, SIDE, SIDE, C), 1.0, 6.0, ((0, 4), (1, 2), (2, 4))),
        "out_grad": scatter_about(seeds[1], (IMAGES, SIDE, SIDE, C), 1.0, 6.0, ((0, 4), (1, 2), (2, 4))),
        "keep_mask": plant((jax.random.randint(seeds[2], (IMAGES,), 0, 5) < 4).astype(jnp.int32), jax.random.fold_in(seeds[2], 1), 0, 1),
        "img_counts": ragged_sizes(seeds[3], N_BA, N_BA * (IMG_DEV + 1) // 2 + 1, IMG_DEV, 1).astype(jnp.int32),
        "mats_master": scatter_about(seeds[4], (2, C, HID), C ** -0.5, 0.3125, ((2, 4),), jnp.float32),
        "chan_master": draw_chan_master(jax.random.fold_in(seeds[16], 71), 0),
        "bias_master": scatter_about(seeds[6], (HID,), 0.5, 3.0, ((0, 4),), jnp.float32),
        "mats_moment": scatter_about(seeds[7], (2, C, HID), (0.6 * (IMAGES * SIDE * SIDE) ** 0.5), 1024.0, ((2, 4),), jnp.float32),
        "chan_moment": scatter_about(seeds[8], (NCH, C), (0.6 * (IMAGES * SIDE * SIDE) ** 0.5), 1024.0, ((1, 4),), jnp.float32),
        "bias_moment": scatter_about(seeds[9], (HID,), (0.6 * (IMAGES * SIDE * SIDE) ** 0.5), 1024.0, ((0, 4),), jnp.float32),
        "mats_second": jnp.clip(jnp.exp(math.log(139345.92) - 1.3862944 * jax.random.uniform(seeds[10], (2, C, HID), jnp.float32) ** level_of(seeds[10], (2, C, HID), ((2, 4),), -0.2, 0.2)), 34836.48, 139345.92),
        "chan_second": jnp.clip(jnp.exp(math.log(139345.92) - 1.3862944 * jax.random.uniform(seeds[11], (NCH, C), jnp.float32) ** level_of(seeds[11], (NCH, C), ((1, 4),), -0.2, 0.2)), 34836.48, 139345.92),
        "bias_second": jnp.clip(jnp.exp(math.log(139345.92) - 1.3862944 * jax.random.uniform(seeds[12], (HID,), jnp.float32) ** level_of(seeds[12], (HID,), ((0, 4),), -0.2, 0.2)), 34836.48, 139345.92),
        "mats_average": scatter_about(seeds[13], (2, C, HID), C ** -0.5, 0.3125, ((2, 4),), jnp.float32),
        "chan_average": draw_chan_average(jax.random.fold_in(seeds[16], 71), 0),
        "bias_average": scatter_about(seeds[15], (HID,), 0.5, 3.0, ((0, 4),), jnp.float32),
    }


@jax.custom_vjp
def low(v):
    return lax.optimization_barrier(v.astype(jnp.bfloat16)).astype(jnp.float32)

@jax.custom_vjp
def low_back(v):
    return v

def low_keep(v):
    return (low(v), None)

def low_pass(kept, grad):
    return (grad,)

def back_keep(v):
    return (v, None)

def back_low(kept, grad):
    return (low(grad),)
low.defvjp(low_keep, low_pass)
low_back.defvjp(back_keep, back_low)

def exact_gelu(value):
    return jax.nn.gelu(value, approximate=False)

def block(image, params, gate):
    mats, chan, bias = params
    mats = low(mats)
    chan = low(chan)
    bias = low(bias)
    reach = KS // 2
    first = KS * KS
    padded = jnp.pad(image, ((0, 0), (reach, reach), (reach, reach), (0, 0)))
    conv = jnp.zeros_like(image)
    for i in range(KS):
        for j in range(KS):
            conv = conv + chan[i * KS + j] * padded[:, i:i + SIDE, j:j + SIDE, :]
    conv = low_back(conv + chan[first])
    center = conv - lax.optimization_barrier(jnp.mean(conv, axis=-1, keepdims=True))
    normed = center * lax.rsqrt(lax.optimization_barrier(jnp.mean(center * center, axis=-1, keepdims=True)) + 1e-06)
    normed_low = low(normed * chan[first + 1] + chan[first + 2])
    hidden_pre = jnp.einsum('nhwc,cf->nhwf', normed_low, mats[0], precision=lax.Precision.HIGHEST) + bias
    hidden_pre = low_back(hidden_pre)
    activated = low(exact_gelu(hidden_pre))
    branch = jnp.einsum('nhwf,cf->nhwc', activated, mats[1], precision=lax.Precision.HIGHEST) + chan[first + 3]
    branch = low_back(branch)
    return image + gate[:, None, None, None] * chan[first + 4] * branch

def adam_step(master, grad, moment, second, average, rate):
    moment_new = 0.5 * moment + 0.5 * grad
    second_new = 0.5 * second + 0.5 * grad * grad
    correct = 1.0 - 0.5 ** STEP
    master_new = master - rate * (moment_new / correct / (jnp.sqrt(second_new / correct) + 1e-08) + 0.05 * master)
    average_new = 0.9 * average + 0.1 * master_new
    return (master_new, moment_new, second_new, average_new)

def reference(images, out_grad, keep_mask, img_counts, mats_master, chan_master, bias_master, mats_moment, chan_moment, bias_moment, mats_second, chan_second, bias_second, mats_average, chan_average, bias_average):
    params = (mats_master, chan_master, bias_master)
    image_groups = images.reshape(N_BA, IMG_DEV, SIDE, SIDE, C)
    grad_groups = out_grad.reshape(N_BA, IMG_DEV, SIDE, SIDE, C)
    keep_groups = keep_mask.reshape(N_BA, IMG_DEV)

    def group(totals, item):
        image, upstream, keeps, count = item
        slots = jnp.arange(IMG_DEV, dtype=jnp.int32) < count
        gate = jnp.where(slots, keeps, 0).astype(jnp.float32)

        def forward(value, weights):
            return block(value, weights, gate)
        result, pull = jax.vjp(forward, image.astype(jnp.float32), params)
        image_grad, param_grads = pull(upstream.astype(jnp.float32))
        totals = jax.tree.map(lambda a, b: a + b, totals, param_grads)
        return (totals, (result.astype(jnp.bfloat16), image_grad.astype(jnp.bfloat16)))
    start = jax.tree.map(jnp.zeros_like, params)
    grads, (results, image_grads) = lax.scan(group, start, (image_groups, grad_groups, keep_groups, img_counts))
    mats_grad, chan_grad, bias_grad = grads
    mats_new, mats_moment_new, mats_second_new, mats_average_new = adam_step(mats_master, mats_grad, mats_moment, mats_second, mats_average, 0.03)
    chan_new, chan_moment_new, chan_second_new, chan_average_new = adam_step(chan_master, chan_grad, chan_moment, chan_second, chan_average, 0.3)
    bias_new, bias_moment_new, bias_second_new, bias_average_new = adam_step(bias_master, bias_grad, bias_moment, bias_second, bias_average, 0.3)
    outputs = results.reshape(IMAGES, SIDE, SIDE, C)
    input_grad = image_grads.reshape(IMAGES, SIDE, SIDE, C)
    return (outputs, input_grad, mats_grad, chan_grad, bias_grad, mats_new, chan_new, bias_new, mats_moment_new, chan_moment_new, bias_moment_new, mats_second_new, chan_second_new, bias_second_new, mats_average_new, chan_average_new, bias_average_new, mats_new.astype(jnp.bfloat16), chan_new.astype(jnp.bfloat16), bias_new.astype(jnp.bfloat16))
```

```python
import functools
import jax
import jax.numpy as jnp
from jax import lax
from jax.experimental import pallas as pl
from jax.experimental.pallas import tpu as pltpu
from jax.sharding import PartitionSpec as P

STEP = 3
C=384; HID=1536; KS=7; R=3
F32=jnp.float32; BF=jnp.bfloat16

def conv_pair(xf, k_ref, cb_ref, z_ref, h, zr, N, TW):
    def step(t, _):
        ct = t // (N//8); nt = t % (N//8)
        c = pl.ds(pl.multiple_of(ct*128,128),128); n = pl.ds(pl.multiple_of(nt*8,8),8)
        b = jnp.broadcast_to(cb_ref[0:1, c],(8,128))
        acc=[[b]*TW for _ in range(2)]
        for ii in range(KS+1):
            row=[xf[h+ii, w, n, c] for w in range(TW+KS-1)]
            for r in range(2):
                i=ii-r
                if 0<=i<KS:
                    for j in range(KS):
                        kk=k_ref[i*KS+j, pl.ds(0,1), c]
                        for w in range(TW):
                            acc[r][w]=acc[r][w]+row[w+j]*kk
        for r in range(2):
            for w in range(TW):
                z_ref[zr+r, w, n, c]=acc[r][w]
        return 0
    lax.fori_loop(0, 3*(N//8), step, 0)

def widen(x_ref, xf, rows, cols):
    def step(t,_):
        for w in range(cols):
            xf[t, w]=x_ref[t, w].astype(F32)
        return 0
    lax.fori_loop(0, rows, step, 0)

def conv_fwd(xpad, taps, cb):
    HP,WP,N,_=xpad.shape; TH,TW=HP-6,WP-6
    def body(x_ref,k_ref,cb_ref,z_ref,xf):
        g=pl.program_id(0)
        @pl.when(g==0)
        def _(): widen(x_ref,xf,HP,WP)
        conv_pair(xf,k_ref,cb_ref,z_ref,2*g,0,N,TW)
    return pl.pallas_call(body,out_shape=jax.ShapeDtypeStruct((TH,TW,N,C),F32),grid=(TH//2,),
        in_specs=[pl.BlockSpec((HP,WP,N,C),lambda g:(0,0,0,0),pipeline_mode=pl.Buffered(1)),
                  pl.BlockSpec((49,1,C),lambda g:(0,0,0)),pl.BlockSpec((1,C),lambda g:(0,0))],
        out_specs=pl.BlockSpec((2,TW,N,C),lambda g:(g,0,0,0)),
        scratch_shapes=[pltpu.VMEM((HP,WP,N,C),F32)],
        compiler_params=pltpu.CompilerParams(vmem_limit_bytes=60<<20),name="conv_fwd")(xpad,taps.reshape(49,1,C),cb)

def conv_back_row(df, k_ref, x_ref, og_ref, ig_ref, gk, h, hr, N, TW):
    def step(t, _):
        ct = t // (N//8); nt = t % (N//8)
        c = pl.ds(pl.multiple_of(ct*128,128),128); n = pl.ds(pl.multiple_of(nt*8,8),8)
        x=[x_ref[hr, w, n, c].astype(F32) for w in range(TW)]
        acc=[og_ref[hr, w, n, c].astype(F32) for w in range(TW)]
        for i in range(KS):
            row=[df[h+6-i, w, n, c] for w in range(TW+KS-1)]
            for j in range(KS):
                kk=k_ref[i*KS+j, pl.ds(0,1), c]
                s=None
                for w in range(TW):
                    d=row[w+6-j]
                    acc[w]=acc[w]+d*kk
                    p=d*x[w]
                    s=p if s is None else s+p
                gk[i*KS+j,:,c]=gk[i*KS+j,:,c]+s
        for w in range(TW):
            ig_ref[hr, w, n, c]=acc[w].astype(BF)
        return 0
    lax.fori_loop(0, 3*(N//8), step, 0)

def conv_back(dzpad, x, og, taps):
    HP,WP,N,_=dzpad.shape; TH,TW=HP-6,WP-6
    def body(d_ref,k_ref,x_ref,og_ref,ig_ref,gk_ref,df,gk):
        g=pl.program_id(0)
        @pl.when(g==0)
        def _():
            widen(d_ref,df,HP,WP)
            gk[...]=jnp.zeros_like(gk)
        conv_back_row(df,k_ref,x_ref,og_ref,ig_ref,gk,g,0,N,TW)
        @pl.when(g==pl.num_programs(0)-1)
        def _(): gk_ref[...]=jnp.sum(gk[...],axis=1)
    return pl.pallas_call(body,out_shape=(jax.ShapeDtypeStruct((TH,TW,N,C),BF),jax.ShapeDtypeStruct((49,C),F32)),grid=(TH,),
        in_specs=[pl.BlockSpec((HP,WP,N,C),lambda g:(0,0,0,0),pipeline_mode=pl.Buffered(1)),
                  pl.BlockSpec((49,1,C),lambda g:(0,0,0)),
                  pl.BlockSpec((1,TW,N,C),lambda g:(g,0,0,0)),pl.BlockSpec((1,TW,N,C),lambda g:(g,0,0,0))],
        out_specs=(pl.BlockSpec((1,TW,N,C),lambda g:(g,0,0,0)),pl.BlockSpec((49,C),lambda g:(0,0))),
        scratch_shapes=[pltpu.VMEM((HP,WP,N,C),F32),pltpu.VMEM((49,8,C),F32)],
        compiler_params=pltpu.CompilerParams(vmem_limit_bytes=60<<20),name="conv_back")(dzpad,taps.reshape(49,1,C),x,og)

P0=0.3275911; A1=0.254829592; A2=-0.284496736; A3=1.421413741; A4=-1.453152027; A5=1.061405429
def gelu_pair(v):
    s=0.7071067811865476
    a=jnp.abs(v)
    t=1.0/(1.0+(P0*s)*a)
    e=jnp.exp(v*v*-0.5)
    q=t*(0.5*A1+t*(0.5*A2+t*(0.5*A3+t*(0.5*A4+t*(0.5*A5)))))*e
    phi=jnp.where(v>0,1.0-q,q)
    return v*phi, phi+v*e*0.3989422804014327

def dg(a,b,ca,cb): return lax.dot_general(a,b,(((ca,),(cb,)),((),())),preferred_element_type=F32)

def mlp_block(z, og, xc, gate, wi, wo, bi_ref, ch_ref, outs, acc, HC):
    gain=ch_ref[1:2]; shift=ch_ref[2:3]; bo=ch_ref[3:4]; ls=ch_ref[4:5]
    out_ref,dz_ref=outs; gwi,gwo,gch,gbi=acc
    mu=jnp.mean(z,axis=1,keepdims=True)
    zc=z-mu
    inv=lax.rsqrt(jnp.mean(zc*zc,axis=1,keepdims=True)+1e-6)
    xhat=zc*inv
    xn=(xhat*gain+shift).astype(BF)
    gog=gate*og.astype(F32)
    db=(gog*ls).astype(BF)
    M=z.shape[0]
    branch=jnp.zeros((M,C),F32); dxn=jnp.zeros((M,C),F32)
    for j in range(HID//HC):
        hs=slice(j*HC,(j+1)*HC)
        pre=dg(xn,wi[:,hs],1,0)+bi_ref[0:1,hs]
        da=dg(db,wo[:,hs],1,0)
        act,gp=gelu_pair(pre)
        act=act.astype(BF)
        dpre32=da*gp
        dpre=dpre32.astype(BF)
        branch+=dg(act,wo[:,hs],1,1)
        dxn+=dg(dpre,wi[:,hs],1,1)
        gwo[:,hs]+=dg(db,act,0,0)
        gwi[:,hs]+=dg(xn,dpre,0,0)
        gbi[:,hs]+=jnp.sum(dpre.astype(F32).reshape(M//8,8,HC),axis=0)
    branch+=bo
    out_ref[...]=(xc.astype(F32)+gate*ls*branch).astype(BF)
    q=dxn*gain
    m1=jnp.mean(q,axis=1,keepdims=True); m2=jnp.mean(q*xhat,axis=1,keepdims=True)
    dz=(inv*(q-m1-xhat*m2)).astype(BF)
    dz_ref[...]=dz
    red=lambda v: jnp.sum(v.reshape(M//8,8,C),axis=0)
    gch[0]+=red(dz.astype(F32)); gch[1]+=red(dxn*xhat); gch[2]+=red(dxn)
    gch[3]+=red(db.astype(F32)); gch[4]+=red(gog*branch)

def mlp(z, og, xc, gate, wi, wo, bi, ch, steps=6, HC=512):
    rows=z.shape[0]; M=rows//steps
    def body(z_ref,og_ref,xc_ref,g_ref,wi_ref,wo_ref,bi_ref,ch_ref,out_ref,dz_ref,gwi_ref,gwo_ref,gch_ref,gbi_ref,gch,gbi):
        s=pl.program_id(0)
        @pl.when(s==0)
        def _():
            gwi_ref[...]=jnp.zeros_like(gwi_ref); gwo_ref[...]=jnp.zeros_like(gwo_ref)
            gch[...]=jnp.zeros_like(gch); gbi[...]=jnp.zeros_like(gbi)
        mlp_block(z_ref[...],og_ref[...],xc_ref[...],g_ref[:,0:1],wi_ref,wo_ref,bi_ref,ch_ref,(out_ref,dz_ref),(gwi_ref,gwo_ref,gch,gbi),HC)
        @pl.when(s==steps-1)
        def _():
            gch_ref[...]=jnp.sum(gch[...],axis=1); gbi_ref[...]=jnp.sum(gbi[...],axis=0,keepdims=True)
    full=lambda *sh: pl.BlockSpec(sh,lambda s:(0,)*len(sh))
    blk=pl.BlockSpec((M,C),lambda s:(s,0))
    return pl.pallas_call(body,out_shape=(jax.ShapeDtypeStruct((rows,C),BF),jax.ShapeDtypeStruct((rows,C),BF),
            jax.ShapeDtypeStruct((C,HID),F32),jax.ShapeDtypeStruct((C,HID),F32),jax.ShapeDtypeStruct((8,C),F32),jax.ShapeDtypeStruct((1,HID),F32)),
        grid=(steps,),in_specs=[blk,blk,blk,full(M,128),full(C,HID),full(C,HID),full(1,HID),full(8,C)],
        out_specs=(blk,blk,full(C,HID),full(C,HID),full(8,C),full(1,HID)),
        scratch_shapes=[pltpu.VMEM((8,8,C),F32),pltpu.VMEM((8,HID),F32)],
        compiler_params=pltpu.CompilerParams(vmem_limit_bytes=62<<20),name="mlp")(z,og,xc,gate,wi,wo,bi,ch)


def with_halo(cells, sides, width):
    for axis, dim in sides:
        count = lax.axis_size(axis)
        ends = count - 1
        head = lax.slice_in_dim(cells, 0, width, axis=dim)
        tail = lax.slice_in_dim(cells, cells.shape[dim] - width, cells.shape[dim], axis=dim)
        cells = jnp.concatenate(
            [
                lax.ppermute(tail, axis, [(i, (i + 1) % count) for i in range(ends)]),
                cells,
                lax.ppermute(head, axis, [((i + 1) % count, i) for i in range(ends)]),
            ],
            axis=dim,
        )
    return cells


def adam_step(master, grad, moment, second, average, rate):
    moment_new = 0.5 * moment + 0.5 * grad
    second_new = 0.5 * second + 0.5 * grad * grad
    correct = 1.0 - 0.5**STEP
    master_new = master - rate * (
        moment_new / correct / (jnp.sqrt(second_new / correct) + 1e-08) + 0.05 * master
    )
    average_new = 0.9 * average + 0.1 * master_new
    return (master_new, moment_new, second_new, average_new)


def local(
    images,
    out_grad,
    keep_mask,
    img_counts,
    mats_master,
    chan_master,
    bias_master,
    mats_moment,
    chan_moment,
    bias_moment,
    mats_second,
    chan_second,
    bias_second,
    mats_average,
    chan_average,
    bias_average,
):
    n_img, rows, cols = images.shape[0], images.shape[1], images.shape[2]
    slots = -(-n_img // 16) * 16
    mats_all, chan_all, bias_all = (
        lax.all_gather(mats_master.astype(BF), "ba", axis=2, tiled=True),
        lax.all_gather(chan_master.astype(BF), "ba", axis=1, tiled=True),
        lax.all_gather(bias_master.astype(BF), "ba", axis=0, tiled=True),
    )
    chan_vals = chan_all.astype(F32)
    taps, rest = chan_vals[:49], jnp.pad(chan_vals[49:], ((0, 3), (0, 0)))
    fill = jnp.arange(n_img, dtype=jnp.int32) < img_counts[0]
    gate = jnp.pad(jnp.where(fill, keep_mask, 0).astype(F32), (0, slots - n_img))
    steps = rows // 2
    gate = jnp.broadcast_to(jnp.tile(gate, 2 * cols)[:, None], (2 * cols * slots, 128))
    pad = ((0, 0), (0, 0), (0, slots - n_img), (0, 0))
    x = jnp.pad(images.transpose(1, 2, 0, 3), pad)
    up = jnp.pad(out_grad.transpose(1, 2, 0, 3), pad)
    halo = (("ha", 0), ("wa", 1))
    z = conv_fwd(with_halo(x, halo, R), taps, rest[:1])
    flat = lambda v: v.reshape(-1, C)
    out, dz, grad_win, grad_wout, gch, gbi = mlp(
        flat(z), flat(up), flat(x), gate, mats_all[0], mats_all[1], bias_all.astype(F32)[None], rest, steps
    )
    dzp = with_halo(dz.reshape(rows, cols, slots, C), halo, R)
    ig, grad_taps = conv_back(dzp, x, up, taps)
    back = lambda v: v.reshape(rows, cols, slots, C)[:, :, :n_img].transpose(2, 0, 1, 3)
    outputs, input_grad = back(out), back(ig)
    mats_local = jnp.stack([grad_win, grad_wout], axis=0)
    chan_local = jnp.concatenate([grad_taps, gch[:5]], axis=0)
    grad_hbias = gbi[0]
    whole = lax.psum((mats_local, chan_local, grad_hbias), ("ha", "wa"))
    mats_grad, chan_grad, bias_grad = (
        lax.psum_scatter(whole[0], "ba", scatter_dimension=2, tiled=True),
        lax.psum_scatter(whole[1], "ba", scatter_dimension=1, tiled=True),
        lax.psum_scatter(whole[2], "ba", scatter_dimension=0, tiled=True),
    )
    mats_new, mats_moment_new, mats_second_new, mats_average_new = adam_step(
        mats_master, mats_grad, mats_moment, mats_second, mats_average, 0.03
    )
    chan_new, chan_moment_new, chan_second_new, chan_average_new = adam_step(
        chan_master, chan_grad, chan_moment, chan_second, chan_average, 0.3
    )
    bias_new, bias_moment_new, bias_second_new, bias_average_new = adam_step(
        bias_master, bias_grad, bias_moment, bias_second, bias_average, 0.3
    )
    return (
        outputs,
        input_grad,
        mats_grad,
        chan_grad,
        bias_grad,
        mats_new,
        chan_new,
        bias_new,
        mats_moment_new,
        chan_moment_new,
        bias_moment_new,
        mats_second_new,
        chan_second_new,
        bias_second_new,
        mats_average_new,
        chan_average_new,
        bias_average_new,
        mats_new.astype(jnp.bfloat16),
        chan_new.astype(jnp.bfloat16),
        bias_new.astype(jnp.bfloat16),
    )


def solution(mesh):
    return jax.shard_map(
        local,
        mesh=mesh,
        in_specs=(
            P("ba", "ha", "wa", None),
            P("ba", "ha", "wa", None),
            P("ba"),
            P("ba"),
            P(None, None, "ba"),
            P(None, "ba"),
            P("ba"),
            P(None, None, "ba"),
            P(None, "ba"),
            P("ba"),
            P(None, None, "ba"),
            P(None, "ba"),
            P("ba"),
            P(None, None, "ba"),
            P(None, "ba"),
            P("ba"),
        ),
        out_specs=(
            P("ba", "ha", "wa", None),
            P("ba", "ha", "wa", None),
            P(None, None, "ba"),
            P(None, "ba"),
            P("ba"),
            P(None, None, "ba"),
            P(None, "ba"),
            P("ba"),
            P(None, None, "ba"),
            P(None, "ba"),
            P("ba"),
            P(None, None, "ba"),
            P(None, "ba"),
            P("ba"),
            P(None, None, "ba"),
            P(None, "ba"),
            P("ba"),
            P(None, None, "ba"),
            P(None, "ba"),
            P("ba"),
        ),
        check_vma=False,
    )
```

```python
import functools

import jax
import jax.numpy as jnp
from jax import lax
from jax.experimental import pallas as pl
from jax.experimental.pallas import tpu as pltpu
from jax.sharding import PartitionSpec as P

C = 384
HID = 1536
KS = 7
R = KS // 2
STEP = 3
F32 = jnp.float32
BF = jnp.bfloat16


MESH = pl.DeviceIdType.MESH


def conv_group(xf, k_ref, cb_ref, z_ref):
    rows, cols = z_ref.shape[0], z_ref.shape[1]

    def step(t, _):
        hp = t // 3
        c = pl.ds(pl.multiple_of((t % 3) * 128, 128), 128)
        base = jnp.broadcast_to(cb_ref[0:1, c], (8, 128))
        acc = [[base] * cols for _ in range(2)]
        for ii in range(KS + 1):
            row = [xf[2 * hp + ii, w, :, c] for w in range(cols + KS - 1)]
            for r in range(2):
                i = ii - r
                if 0 <= i < KS:
                    for j in range(KS):
                        tap = k_ref[i * KS + j, :, c]
                        for w in range(cols):
                            acc[r][w] = acc[r][w] + row[w + j] * tap
        for r in range(2):
            for w in range(cols):
                z_ref[2 * hp + r, w, :, c] = acc[r][w]
        return 0

    lax.fori_loop(0, rows // 2 * 3, step, 0)


def conv_back_group(df, k_ref, xp, og, ig, gk, g):
    rows, cols = ig.shape[1], ig.shape[2]

    def step(t, _):
        h = t // 3
        c = pl.ds(pl.multiple_of((t % 3) * 128, 128), 128)
        x = [xp[g, h + R, w + R, :, c].astype(F32) for w in range(cols)]
        acc = [og[g, h, w, :, c].astype(F32) for w in range(cols)]
        for i in range(KS):
            row = [df[h + KS - 1 - i, w, :, c] for w in range(cols + KS - 1)]
            for j in range(KS):
                tap = k_ref[i * KS + j, :, c]
                part = None
                for w in range(cols):
                    d = row[w + KS - 1 - j]
                    acc[w] = acc[w] + d * tap
                    part = d * x[w] if part is None else part + d * x[w]
                gk[i * KS + j, :, c] = gk[i * KS + j, :, c] + part
        for w in range(cols):
            ig[g, h, w, :, c] = acc[w].astype(BF)
        return 0

    lax.fori_loop(0, rows * 3, step, 0)


def widen(src, g, dst):
    def step(t, _):
        for w in range(dst.shape[1]):
            dst[t, w] = src[g, t, w].astype(F32)
        return 0

    lax.fori_loop(0, dst.shape[0], step, 0)


def gelu_pair(v):
    t = 1.0 / (1.0 + (0.3275911 * 0.7071067811865476) * jnp.abs(v))
    e = jnp.exp(v * v * -0.5)
    tail = t * (0.127414796 + t * (-0.142248368 + t * (0.7107068705 + t * (-0.7265760135 + t * 0.5307027145)))) * e
    phi = jnp.where(v > 0, 1.0 - tail, tail)
    return v * phi, phi + v * e * 0.3989422804014327


def dg(a, b, ca, cb):
    return lax.dot_general(a, b, (((ca,), (cb,)), ((), ())), preferred_element_type=F32)


def mlp_group(z_ref, og, xp, gate_ref, wi, wo, bi_ref, ch_ref, out, dzp, gwi, gwo, gch, gbi, g):
    rows, cols = z_ref.shape[0], z_ref.shape[1]
    m = rows * cols * 8
    flat = lambda v: v.reshape(m, C)
    cube = lambda v: v.reshape(rows, cols, 8, C)
    gain, shift, bo, ls = (ch_ref[k : k + 1] for k in range(1, 5))
    z = flat(z_ref[...])
    zc = z - jnp.mean(z, axis=1, keepdims=True)
    inv = lax.rsqrt(jnp.mean(zc * zc, axis=1, keepdims=True) + 1e-6)
    xhat = zc * inv
    xn = (xhat * gain + shift).astype(BF)
    gate = gate_ref[g]
    gog = flat(og[g].astype(F32) * gate)
    db = (gog * ls).astype(BF)
    branch = jnp.zeros((m, C), F32)
    dxn = jnp.zeros((m, C), F32)
    for j in range(HID // HC):
        hs = slice(j * HC, (j + 1) * HC)
        pre = dg(xn, wi[:, hs], 1, 0) + bi_ref[0:1, hs]
        da = dg(db, wo[:, hs], 1, 0)
        act, slope = gelu_pair(pre)
        act = act.astype(BF)
        dpre = (da * slope).astype(BF)
        branch += dg(act, wo[:, hs], 1, 1)
        dxn += dg(dpre, wi[:, hs], 1, 1)
        gwo[:, hs] += dg(db, act, 0, 0)
        gwi[:, hs] += dg(xn, dpre, 0, 0)
        gbi[:, hs] += jnp.sum(dpre.astype(F32).reshape(m // 8, 8, HC), axis=0)
    branch += bo
    mid = (slice(R, R + rows), slice(R, R + cols))
    out[g] = (xp[(g, *mid)].astype(F32) + cube(ls * branch) * gate).astype(BF)
    q = dxn * gain
    m1 = jnp.mean(q, axis=1, keepdims=True)
    m2 = jnp.mean(q * xhat, axis=1, keepdims=True)
    dz = (inv * (q - m1 - xhat * m2)).astype(BF)
    dzp[(g, *mid)] = cube(dz)
    red = lambda v: jnp.sum(v.reshape(m // 8, 8, C), axis=0)
    gch[0] += red(dz.astype(F32))
    gch[1] += red(dxn * xhat)
    gch[2] += red(dxn)
    gch[3] += red(db.astype(F32))
    gch[4] += red(gog * branch)


HC = 512


def exchange(n_wa, rows, cols, pad, cs, cr, rs, rr):
    w = lax.axis_index("wa")
    a = lax.axis_index("ha")
    own = slice(R, R + rows)

    def to_left(g, src=None):
        src = pad.at[g, own, R : 2 * R] if src is None else src
        return pltpu.make_async_remote_copy(
            src, pad.at[g, own, R + cols :], cs.at[g, 0], cr.at[g, 0], device_id={"wa": w - 1}, device_id_type=MESH
        )

    def to_right(g, src=None):
        src = pad.at[g, own, cols : cols + R] if src is None else src
        return pltpu.make_async_remote_copy(
            src, pad.at[g, own, :R], cs.at[g, 1], cr.at[g, 1], device_id={"wa": w + 1}, device_id_type=MESH
        )

    def rows_to(g, up):
        src = pad.at[g, R : 2 * R] if up else pad.at[g, rows : rows + R]
        dst = pad.at[g, R + rows :] if up else pad.at[g, :R]
        return pltpu.make_async_remote_copy(
            src, dst, rs.at[g], rr.at[g], device_id={"ha": 1 - a}, device_id_type=MESH
        )

    def both(g, f0, f1):
        pl.when(a == 0)(lambda: f0(rows_to(g, False)))
        pl.when(a == 1)(lambda: f1(rows_to(g, True)))

    def start_cols(g, left=None, right=None):
        pl.when(w > 0)(lambda: to_left(g, left).start())
        pl.when(w < n_wa - 1)(lambda: to_right(g, right).start())

    def wait_cols(g):
        pl.when(w < n_wa - 1)(lambda: to_left(g).wait_recv())
        pl.when(w > 0)(lambda: to_right(g).wait_recv())

    def start_rows(g):
        both(g, lambda c: c.start(), lambda c: c.start())

    def wait_rows(g):
        rows_to(g, True).wait_recv()

    def drain(g):
        pl.when(w > 0)(lambda: to_left(g).wait_send())
        pl.when(w < n_wa - 1)(lambda: to_right(g).wait_send())
        rows_to(g, True).wait_send()

    def zero_edges(g):
        z = lambda h, v: jnp.zeros((h, v, 8, C), BF)
        pl.when(w == 0)(lambda: pad.__setitem__((g, own, slice(0, R)), z(rows, R)))
        pl.when(w == n_wa - 1)(lambda: pad.__setitem__((g, own, slice(R + cols, 2 * R + cols)), z(rows, R)))
        pl.when(a == 0)(lambda: pad.__setitem__((g, slice(0, R)), z(R, cols + 2 * R)))
        pl.when(a == 1)(lambda: pad.__setitem__((g, slice(R + rows, 2 * R + rows)), z(R, cols + 2 * R)))

    return start_cols, wait_cols, start_rows, wait_rows, drain, zero_edges


def main_kernel(
    n_wa, x_hbm, og_hbm, gate_ref, k_ref, ch_ref, bi_ref, wi, wo,
    out, ig, gwi, gwo, gch_out, gbi_out, gk_out,
    xp, dzp, og, xf, z, gch, gbi, gk,
    xcs, xcr, xrs, xrr, dcs, dcr, drs, drr, own_sem, og_sem,
):
    groups, rows, cols = x_hbm.shape[0], x_hbm.shape[1], x_hbm.shape[2]
    w = lax.axis_index("wa")
    a = lax.axis_index("ha")
    mid = (slice(R, R + rows), slice(R, R + cols))
    xh = exchange(n_wa, rows, cols, xp, xcs, xcr, xrs, xrr)
    dh = exchange(n_wa, rows, cols, dzp, dcs, dcr, drs, drr)
    own = lambda g: pltpu.make_async_copy(x_hbm.at[g], xp.at[(g, *mid)], own_sem.at[g])
    ogc = lambda g: pltpu.make_async_copy(og_hbm.at[g], og.at[g], og_sem.at[g])

    barrier = pltpu.get_barrier_semaphore()
    pl.when(w > 0)(lambda: pl.semaphore_signal(barrier, inc=1, device_id={"wa": w - 1}, device_id_type=MESH))
    pl.when(w < n_wa - 1)(lambda: pl.semaphore_signal(barrier, inc=1, device_id={"wa": w + 1}, device_id_type=MESH))
    pl.semaphore_signal(barrier, inc=1, device_id={"ha": 1 - a}, device_id_type=MESH)
    for g in range(groups):
        own(g).start()
        ogc(g).start()
    near = jnp.where(w > 0, 1, 0) + jnp.where(w < n_wa - 1, 1, 0) + 1
    pl.semaphore_wait(barrier, near)

    def loop(n, f):
        lax.fori_loop(0, n, lambda g, _: (f(g), 0)[1], 0)

    loop(groups, lambda g: xh[0](g, x_hbm.at[g, :, 0:R], x_hbm.at[g, :, cols - R : cols]))
    loop(groups, lambda g: (xh[5](g), dh[5](g)))
    gwi[...] = jnp.zeros_like(gwi)
    gwo[...] = jnp.zeros_like(gwo)
    gch[...] = jnp.zeros_like(gch)
    gbi[...] = jnp.zeros_like(gbi)
    gk[...] = jnp.zeros_like(gk)

    def ready(g):
        own(g).wait()
        xh[1](g)
        xh[2](g)

    ready(0)

    def forward(g):
        pl.when(g + 1 < groups)(lambda: ready(g + 1))
        xh[3](g)
        ogc(g).wait()
        widen(xp, g, xf)
        conv_group(xf, k_ref, ch_ref, z)
        mlp_group(z, og, xp, gate_ref, wi, wo, bi_ref, ch_ref, out, dzp, gwi, gwo, gch, gbi, g)
        dh[0](g)

    loop(groups, forward)

    def ready_back(g):
        dh[1](g)
        dh[2](g)

    ready_back(0)

    def backward(g):
        pl.when(g + 1 < groups)(lambda: ready_back(g + 1))
        dh[3](g)
        widen(dzp, g, xf)
        conv_back_group(xf, k_ref, xp, og, ig, gk, g)

    loop(groups, backward)
    gch_out[...] = jnp.sum(gch[...], axis=1)
    gbi_out[...] = jnp.sum(gbi[...], axis=0, keepdims=True)
    gk_out[...] = jnp.sum(gk[...], axis=1)
    loop(groups, lambda g: (xh[4](g), dh[4](g)))


def run_main(n_wa, x, og, gate, taps, ch, bi, wi, wo):
    groups, rows, cols = x.shape[:3]
    hbm = pl.BlockSpec(memory_space=pl.ANY)
    vm = pl.BlockSpec(memory_space=pltpu.VMEM)
    big = (groups, rows + 2 * R, cols + 2 * R, 8, C)
    dma = pltpu.SemaphoreType.DMA
    S = jax.ShapeDtypeStruct
    return pl.pallas_call(
        functools.partial(main_kernel, n_wa),
        out_shape=(S(x.shape, BF), S(x.shape, BF), S((C, HID), F32), S((C, HID), F32), S((8, C), F32), S((1, HID), F32), S((49, C), F32)),
        in_specs=[hbm, hbm] + [vm] * 6,
        out_specs=(vm,) * 7,
        scratch_shapes=[
            pltpu.VMEM(big, BF), pltpu.VMEM(big, BF), pltpu.VMEM(x.shape, BF),
            pltpu.VMEM(big[1:], F32), pltpu.VMEM((rows, cols, 8, C), F32),
            pltpu.VMEM((8, 8, C), F32), pltpu.VMEM((8, HID), F32), pltpu.VMEM((49, 8, C), F32),
            dma((groups, 2)), dma((groups, 2)), dma((groups,)), dma((groups,)),
            dma((groups, 2)), dma((groups, 2)), dma((groups,)), dma((groups,)),
            dma((groups,)), dma((groups,)),
        ],
        compiler_params=pltpu.CompilerParams(collective_id=0, has_side_effects=True, vmem_limit_bytes=67043328),
        name="main",
    )(x, og, gate, taps, ch, bi, wi, wo)


def adam_step(master, grad, moment, second, average, rate):
    moment_new = 0.5 * moment + 0.5 * grad
    second_new = 0.5 * second + 0.5 * grad * grad
    correct = 1.0 - 0.5**STEP
    master_new = master - rate * (
        moment_new / correct / (jnp.sqrt(second_new / correct) + 1e-08) + 0.05 * master
    )
    average_new = 0.9 * average + 0.1 * master_new
    return (master_new, moment_new, second_new, average_new)


def local(
    images,
    out_grad,
    keep_mask,
    img_counts,
    mats_master,
    chan_master,
    bias_master,
    mats_moment,
    chan_moment,
    bias_moment,
    mats_second,
    chan_second,
    bias_second,
    mats_average,
    chan_average,
    bias_average,
):
    n_img, rows, cols = images.shape[0], images.shape[1], images.shape[2]
    groups = -(-n_img // 8)
    slots = groups * 8
    mats_all, chan_all, bias_all = (
        lax.all_gather(mats_master.astype(BF), "ba", axis=2, tiled=True),
        lax.all_gather(chan_master.astype(BF), "ba", axis=1, tiled=True),
        lax.all_gather(bias_master.astype(BF), "ba", axis=0, tiled=True),
    )
    chan_vals = chan_all.astype(F32)
    taps, rest = chan_vals[:49], jnp.pad(chan_vals[49:], ((0, 3), (0, 0)))
    fill = jnp.arange(n_img, dtype=jnp.int32) < img_counts[0]
    gate = jnp.pad(jnp.where(fill, keep_mask, 0).astype(F32), (0, slots - n_img))
    gate = jnp.broadcast_to(gate.reshape(groups, 8, 1), (groups, 8, C))

    def grouped(v):
        v = jnp.pad(v.transpose(1, 2, 0, 3), ((0, 0), (0, 0), (0, slots - n_img), (0, 0)))
        return v.reshape(rows, cols, groups, 8, C).transpose(2, 0, 1, 3, 4)

    out, ig, grad_win, grad_wout, gch, gbi, grad_taps = run_main(
        lax.axis_size("wa"), grouped(images), grouped(out_grad), gate, taps[:, None],
        rest, bias_all.astype(F32)[None], mats_all[0], mats_all[1],
    )
    back = lambda v: v.transpose(1, 2, 0, 3, 4).reshape(rows, cols, slots, C)[:, :, :n_img].transpose(2, 0, 1, 3)
    outputs, input_grad = back(out), back(ig)
    mats_local = jnp.stack([grad_win, grad_wout], axis=0)
    chan_local = jnp.concatenate([grad_taps, gch[:5]], axis=0)
    grad_hbias = gbi[0]
    whole = lax.psum((mats_local, chan_local, grad_hbias), ("ha", "wa"))
    mats_grad, chan_grad, bias_grad = (
        lax.psum_scatter(whole[0], "ba", scatter_dimension=2, tiled=True),
        lax.psum_scatter(whole[1], "ba", scatter_dimension=1, tiled=True),
        lax.psum_scatter(whole[2], "ba", scatter_dimension=0, tiled=True),
    )
    mats_new, mats_moment_new, mats_second_new, mats_average_new = adam_step(
        mats_master, mats_grad, mats_moment, mats_second, mats_average, 0.03
    )
    chan_new, chan_moment_new, chan_second_new, chan_average_new = adam_step(
        chan_master, chan_grad, chan_moment, chan_second, chan_average, 0.3
    )
    bias_new, bias_moment_new, bias_second_new, bias_average_new = adam_step(
        bias_master, bias_grad, bias_moment, bias_second, bias_average, 0.3
    )
    return (
        outputs,
        input_grad,
        mats_grad,
        chan_grad,
        bias_grad,
        mats_new,
        chan_new,
        bias_new,
        mats_moment_new,
        chan_moment_new,
        bias_moment_new,
        mats_second_new,
        chan_second_new,
        bias_second_new,
        mats_average_new,
        chan_average_new,
        bias_average_new,
        mats_new.astype(jnp.bfloat16),
        chan_new.astype(jnp.bfloat16),
        bias_new.astype(jnp.bfloat16),
    )


def solution(mesh):
    return jax.shard_map(
        local,
        mesh=mesh,
        in_specs=(
            P("ba", "ha", "wa", None),
            P("ba", "ha", "wa", None),
            P("ba"),
            P("ba"),
            P(None, None, "ba"),
            P(None, "ba"),
            P("ba"),
            P(None, None, "ba"),
            P(None, "ba"),
            P("ba"),
            P(None, None, "ba"),
            P(None, "ba"),
            P("ba"),
            P(None, None, "ba"),
            P(None, "ba"),
            P("ba"),
        ),
        out_specs=(
            P("ba", "ha", "wa", None),
            P("ba", "ha", "wa", None),
            P(None, None, "ba"),
            P(None, "ba"),
            P("ba"),
            P(None, None, "ba"),
            P(None, "ba"),
            P("ba"),
            P(None, None, "ba"),
            P(None, "ba"),
            P("ba"),
            P(None, None, "ba"),
            P(None, "ba"),
            P("ba"),
            P(None, None, "ba"),
            P(None, "ba"),
            P("ba"),
            P(None, None, "ba"),
            P(None, "ba"),
            P("ba"),
        ),
        check_vma=False,
    )
```

```python
import functools

import jax
import jax.numpy as jnp
from jax import lax
from jax.experimental import pallas as pl
from jax.experimental.pallas import tpu as pltpu
from jax.sharding import PartitionSpec as P

C = 384
HID = 1536
KS = 7
R = KS // 2
STEP = 3
F32 = jnp.float32
BF = jnp.bfloat16


MESH = pl.DeviceIdType.MESH


def conv_group(xf, ch, z_ref):
    rows, cols = z_ref.shape[0], z_ref.shape[1]

    def step(t, _):
        hp = t // 3
        c = pl.ds(pl.multiple_of((t % 3) * 128, 128), 128)
        base = jnp.broadcast_to(ch[49:50, c], (8, 128))
        acc = [[base] * cols for _ in range(2)]
        for ii in range(KS + 1):
            row = [xf[2 * hp + ii, w, :, c] for w in range(cols + KS - 1)]
            for r in range(2):
                i = ii - r
                if 0 <= i < KS:
                    for j in range(KS):
                        tap = ch[i * KS + j : i * KS + j + 1, c]
                        for w in range(cols):
                            acc[r][w] = acc[r][w] + row[w + j] * tap
        for r in range(2):
            for w in range(cols):
                z_ref[2 * hp + r, w, :, c] = acc[r][w]
        return 0

    lax.fori_loop(0, rows // 2 * 3, step, 0)


def conv_back_group(df, ch, xp, og, ig, gk, g, first, count):
    rows, cols = ig.shape[1], ig.shape[2]

    def step(t, _):
        h = first + t // 3
        c = pl.ds(pl.multiple_of((t % 3) * 128, 128), 128)
        x = [xp[g, h + R, w + R, :, c].astype(F32) for w in range(cols)]
        acc = [og[g, h, w, :, c].astype(F32) for w in range(cols)]
        for i in range(KS):
            row = [df[h + KS - 1 - i, w, :, c] for w in range(cols + KS - 1)]
            for j in range(KS):
                tap = ch[i * KS + j : i * KS + j + 1, c]
                part = None
                for w in range(cols):
                    d = row[w + KS - 1 - j]
                    acc[w] = acc[w] + d * tap
                    part = d * x[w] if part is None else part + d * x[w]
                gk[i * KS + j, :, c] = gk[i * KS + j, :, c] + part
        for w in range(cols):
            ig[g, h, w, :, c] = acc[w].astype(BF)
        return 0

    lax.fori_loop(0, count * 3, step, 0)


def widen(src, g, dst):
    def step(t, _):
        for w in range(dst.shape[1]):
            dst[t, w] = src[g, t, w].astype(F32)
        return 0

    lax.fori_loop(0, dst.shape[0], step, 0)


def gelu_pair(v):
    t = 1.0 / (1.0 + (0.3275911 * 0.7071067811865476) * jnp.abs(v))
    e = jnp.exp(v * v * -0.5)
    tail = t * (0.127414796 + t * (-0.142248368 + t * (0.7107068705 + t * (-0.7265760135 + t * 0.5307027145)))) * e
    phi = jnp.where(v > 0, 1.0 - tail, tail)
    return v * phi, phi + v * e * 0.3989422804014327


def dg(a, b, ca, cb):
    return lax.dot_general(a, b, (((ca,), (cb,)), ((), ())), preferred_element_type=F32)


def mlp_group(z_ref, og, xp, gate_ref, w_all, bi_ref, ch_ref, out, dzp, gw, gch, gbi, g):
    rows, cols = z_ref.shape[0], z_ref.shape[1]
    m = rows * cols * 8
    flat = lambda v: v.reshape(m, C)
    cube = lambda v: v.reshape(rows, cols, 8, C)
    gain, shift, bo, ls = (ch_ref[k : k + 1] for k in range(50, 54))
    z = flat(z_ref[...])
    zc = z - jnp.mean(z, axis=1, keepdims=True)
    inv = lax.rsqrt(jnp.mean(zc * zc, axis=1, keepdims=True) + 1e-6)
    xhat = zc * inv
    xn = (xhat * gain + shift).astype(BF)
    gate = gate_ref[g]
    gog = flat(og[g].astype(F32) * gate)
    db = (gog * ls).astype(BF)
    branch = jnp.zeros((m, C), F32)
    dxn = jnp.zeros((m, C), F32)
    for j in range(HID // HC):
        hs = slice(j * HC, (j + 1) * HC)
        pre = dg(xn, w_all[0, :, hs], 1, 0) + bi_ref[0:1, hs]
        da = dg(db, w_all[1, :, hs], 1, 0)
        act, slope = gelu_pair(pre)
        act = act.astype(BF)
        dpre = (da * slope).astype(BF)
        branch += dg(act, w_all[1, :, hs], 1, 1)
        dxn += dg(dpre, w_all[0, :, hs], 1, 1)
        gw[1, :, hs] += dg(db, act, 0, 0)
        gw[0, :, hs] += dg(xn, dpre, 0, 0)
        gbi[:, hs] += jnp.sum(dpre.astype(F32).reshape(m // 8, 8, HC), axis=0)
    branch += bo
    mid = (slice(R, R + rows), slice(R, R + cols))
    out[g] = (xp[(g, *mid)].astype(F32) + cube(ls * branch) * gate).astype(BF)
    q = dxn * gain
    m1 = jnp.mean(q, axis=1, keepdims=True)
    m2 = jnp.mean(q * xhat, axis=1, keepdims=True)
    dz = (inv * (q - m1 - xhat * m2)).astype(BF)
    dzp[(g, *mid)] = cube(dz)
    red = lambda v: jnp.sum(v.reshape(m // 8, 8, C), axis=0)
    gch[0] += red(dz.astype(F32))
    gch[1] += red(dxn * xhat)
    gch[2] += red(dxn)
    gch[3] += red(db.astype(F32))
    gch[4] += red(gog * branch)


HC = 512


def exchange(n_wa, rows, cols, pad, cs, cr, rs, rr):
    w = lax.axis_index("wa")
    a = lax.axis_index("ha")
    own = slice(R, R + rows)

    def to_left(g, src=None):
        src = pad.at[g, own, R : 2 * R] if src is None else src
        return pltpu.make_async_remote_copy(
            src, pad.at[g, own, R + cols :], cs.at[g, 0], cr.at[g, 0], device_id={"wa": w - 1}, device_id_type=MESH
        )

    def to_right(g, src=None):
        src = pad.at[g, own, cols : cols + R] if src is None else src
        return pltpu.make_async_remote_copy(
            src, pad.at[g, own, :R], cs.at[g, 1], cr.at[g, 1], device_id={"wa": w + 1}, device_id_type=MESH
        )

    def rows_to(g, up):
        src = pad.at[g, R : 2 * R] if up else pad.at[g, rows : rows + R]
        dst = pad.at[g, R + rows :] if up else pad.at[g, :R]
        return pltpu.make_async_remote_copy(
            src, dst, rs.at[g], rr.at[g], device_id={"ha": 1 - a}, device_id_type=MESH
        )

    def both(g, f0, f1):
        pl.when(a == 0)(lambda: f0(rows_to(g, False)))
        pl.when(a == 1)(lambda: f1(rows_to(g, True)))

    def start_cols(g, left=None, right=None):
        pl.when(w > 0)(lambda: to_left(g, left).start())
        pl.when(w < n_wa - 1)(lambda: to_right(g, right).start())

    def wait_cols(g):
        pl.when(w < n_wa - 1)(lambda: to_left(g).wait_recv())
        pl.when(w > 0)(lambda: to_right(g).wait_recv())

    def start_rows(g):
        both(g, lambda c: c.start(), lambda c: c.start())

    def wait_rows(g):
        rows_to(g, True).wait_recv()

    def drain(g):
        pl.when(w > 0)(lambda: to_left(g).wait_send())
        pl.when(w < n_wa - 1)(lambda: to_right(g).wait_send())
        rows_to(g, True).wait_send()

    def zero_edges(g):
        z = lambda h, v: jnp.zeros((h, v, 8, C), BF)
        pl.when(w == 0)(lambda: pad.__setitem__((g, own, slice(0, R)), z(rows, R)))
        pl.when(w == n_wa - 1)(lambda: pad.__setitem__((g, own, slice(R + cols, 2 * R + cols)), z(rows, R)))
        pl.when(a == 0)(lambda: pad.__setitem__((g, slice(0, R)), z(R, cols + 2 * R)))
        pl.when(a == 1)(lambda: pad.__setitem__((g, slice(R + rows, 2 * R + rows)), z(R, cols + 2 * R)))

    return start_cols, wait_cols, start_rows, wait_rows, drain, zero_edges


def place(b, shape, axis):
    whole = lax.broadcasted_iota(jnp.int32, shape, axis)
    part = lax.broadcasted_iota(jnp.int32, shape, 1 - axis)
    return jnp.where((whole == part + b * 96) & (part < 96), 1.0, 0.0).astype(BF)


def remote(src, dst, send, recv, **where):
    return pltpu.make_async_remote_copy(src, dst, send, recv, device_id=where, device_id_type=MESH)


def main_kernel(n_wa, n_ba, *refs):
    inside = n_ba == 4
    it = iter(refs)
    take = lambda n: [next(it) for _ in range(n)]
    x_hbm, og_hbm, gate_ref = take(3)
    if inside:
        mats_hbm, small_hbm = take(2)
    else:
        w_all, ch, bi = take(3)
    out, ig = take(2)
    if inside:
        gf, gsmall = take(2)
    else:
        gw, gch_out, gbi_out, gk_out = take(4)
    xp, dzp, og, xf, z, gch, gbi, gk = take(8)
    xcs, xcr, xrs, xrr, dcs, dcr, drs, drr, own_sem, og_sem = take(10)
    if inside:
        w_all, ch, bi, gw, s_all = take(5)
        s_send, s_recv, w_own, w_up, w_dn, w_recv, w_cs, w_cr = take(8)
        sb, rb, ub, db, ui, di, fin, pb, pi = take(9)
        r_cs, r_cr, u_s, u_r, d_s, d_r, p_s, p_r, q_s, q_r, f_s, f_r = take(12)
        gs, gs_in, gp, gz, gz_out = take(5)
        t_s, t_r, tp_s, tp_r, tz_s, tz_r = take(6)

    groups, rows, cols = x_hbm.shape[0], x_hbm.shape[1], x_hbm.shape[2]
    w = lax.axis_index("wa")
    a = lax.axis_index("ha")
    me = lax.axis_index("ba")
    mid = (slice(R, R + rows), slice(R, R + cols))
    xh = exchange(n_wa, rows, cols, xp, xcs, xcr, xrs, xrr)
    dh = exchange(n_wa, rows, cols, dzp, dcs, dcr, drs, drr)
    own = lambda g: pltpu.make_async_copy(x_hbm.at[g], xp.at[(g, *mid)], own_sem.at[g])
    ogc = lambda g: pltpu.make_async_copy(og_hbm.at[g], og.at[g], og_sem.at[g])

    def loop(n, f):
        lax.fori_loop(0, n, lambda g, _: (f(g), 0)[1], 0)

    def when(cond, f):
        pl.when(cond)(f)

    barrier = pltpu.get_barrier_semaphore()
    greet = lambda **d: pl.semaphore_signal(barrier, inc=1, device_id=d, device_id_type=MESH)
    for g in range(groups):
        own(g).start()
        ogc(g).start()
    greet(ha=1 - a)
    if inside:
        for d in range(1, n_wa):
            greet(wa=lax.rem(w + d, n_wa))
        for d in range(1, n_ba):
            greet(ba=lax.rem(me + d, n_ba))
        pl.semaphore_wait(barrier, n_wa + n_ba - 1)
    else:
        when(w > 0, lambda: greet(wa=w - 1))
        when(w < n_wa - 1, lambda: greet(wa=w + 1))
        pl.semaphore_wait(barrier, jnp.where(w > 0, 1, 0) + jnp.where(w < n_wa - 1, 1, 0) + 1)

    xh[0](0, x_hbm.at[0, :, 0:R], x_hbm.at[0, :, cols - R : cols])
    if inside:
        lanes = lambda s: pl.ds(pl.multiple_of(s * C, C), C)
        shard = lambda h, s: w_all.at[h, :, lanes(s)]
        small_to = lambda d: remote(
            small_hbm, s_all.at[me], s_send.at[d - 1], s_recv.at[me], ba=lax.rem(me + d, n_ba)
        )
        small_from = lambda s: remote(small_hbm, s_all.at[s], s_send.at[0], s_recv.at[s], ba=me)
        w_mine = lambda h: pltpu.make_async_copy(mats_hbm.at[h], shard(h, me), w_own.at[h])
        s_mine = pltpu.make_async_copy(small_hbm, s_all.at[me], w_own.at[2])
        w_up_to = lambda s, src: remote(src, shard(a, s), w_up.at[s], w_recv.at[s], ba=me + 1)
        w_dn_to = lambda s, src: remote(src, shard(a, s), w_dn.at[s], w_recv.at[s], ba=me - 1)
        w_core = lambda s: remote(shard(a, s), shard(a, s), w_cs.at[s], w_cr.at[s], ha=1 - a)
        for d in range(1, n_ba):
            small_to(d).start()
        when(me < n_ba - 1, lambda: w_up_to(me, mats_hbm.at[a]).start())
        when(me > 0, lambda: w_dn_to(me, mats_hbm.at[a]).start())
        s_mine.start()
        w_mine(0).start()
        w_mine(1).start()

        def hop(d):
            def low():
                w_up_to(me - d, shard(a, me - d)).wait_recv()
                when(me < n_ba - 1, lambda: w_up_to(me - d, shard(a, me - d)).start())
                w_core(me - d).start()

            def high():
                w_dn_to(me + d, shard(a, me + d)).wait_recv()
                when(me > 0, lambda: w_dn_to(me + d, shard(a, me + d)).start())
                w_core(me + d).start()

            when(me >= d, low)
            when(me + d < n_ba, high)

    loop(groups - 1, lambda g: xh[0](g + 1, x_hbm.at[g + 1, :, 0:R], x_hbm.at[g + 1, :, cols - R : cols]))
    loop(groups, lambda g: (xh[5](g), dh[5](g)))
    gw[...] = jnp.zeros_like(gw)
    gch[...] = jnp.zeros_like(gch)
    gbi[...] = jnp.zeros_like(gbi)
    gk[...] = jnp.zeros_like(gk)
    if inside:
        s_mine.wait()
        for d in range(1, n_ba):
            small_from(lax.rem(me + d, n_ba)).wait_recv()
        ch[...] = sum(dg(s_all[b], place(b, (128, C), 1), 1, 0) for b in range(n_ba))
        for b in range(n_ba):
            part = s_all[b, 56:64].astype(F32)
            for k in range(3):
                bi[0:1, b * C + k * 128 : b * C + (k + 1) * 128] = part[k : k + 1]

    def ready(g):
        own(g).wait()
        xh[1](g)
        xh[2](g)

    def conv(g):
        when(g + 1 < groups, lambda: ready(g + 1))
        xh[3](g)
        widen(xp, g, xf)
        conv_group(xf, ch, z.at[g % 2])

    ready(0)
    if inside:
        hop(1)
    conv(0)
    if inside:
        hop(2)
    conv(1)
    if inside:
        hop(3)
        w_mine(0).wait()
        w_mine(1).wait()
        for d in range(1, n_ba):
            w_core(lax.rem(me + d, n_ba)).wait_recv()

    def forward(g):
        ogc(g).wait()
        mlp_group(z.at[g % 2], og, xp, gate_ref, w_all, bi, ch, out, dzp, gw, gch, gbi, g)
        dh[0](g)
        when(g + 2 < groups, lambda: conv(g + 2))

    loop(groups, forward)

    actions = []
    if inside:
        part = lambda s: slice(s * C, (s + 1) * C)
        to_core = lambda s: remote(sb.at[s], rb.at[s], r_cs.at[s], r_cr.at[s], ha=1 - a)
        up = lambda s: remote(ub.at[s], ui.at[s], u_s.at[s], u_r.at[s], ba=me + 1)
        down = lambda s: remote(db.at[s], di.at[s], d_s.at[s], d_r.at[s], ba=me - 1)
        mine = lambda s: gw[a, :, part(s)] + rb[s].astype(F32)

        def to_other_core():
            for s in range(n_ba):
                sb[s] = gw[1 - a, :, part(s)].astype(BF)
            for s in range(n_ba):
                to_core(s).start()

        def line(step):
            def run():
                if step == 0:
                    for s in range(n_ba):
                        to_core(s).wait_recv()

                def go_up():
                    for s in range(n_ba - 1, step, -1):
                        if step:
                            up(s).wait_recv()
                        ub[s] = (mine(s) + ui[s].astype(F32) if step else mine(s)).astype(BF)
                        up(s).start()

                def go_down():
                    for s in range(n_ba - 1 - step):
                        if step:
                            down(s).wait_recv()
                        db[s] = (mine(s) + di[s].astype(F32) if step else mine(s)).astype(BF)
                        down(s).start()

                when(me == step, go_up)
                when(me == n_ba - 1 - step, go_down)

            return run

        quarter = C // n_wa
        strip = lambda q: pl.ds(pl.multiple_of(q * quarter, quarter), quarter)
        around = lambda d: lax.rem(w + d, n_wa)
        to_owner = lambda q: remote(pb.at[q], pi.at[w], p_s.at[q], p_r.at[w], wa=q)
        from_peer = lambda q: remote(pb.at[q], pi.at[q], p_s.at[q], p_r.at[q], wa=q)
        spread = lambda q: remote(gf.at[a, strip(w)], gf.at[a, strip(w)], q_s.at[q], q_r.at[w], wa=q)
        gather = lambda q: remote(gf.at[a, strip(q)], gf.at[a, strip(q)], q_s.at[q], q_r.at[q], wa=q)
        swap = lambda: remote(gf.at[a], gf.at[a], f_s, f_r, ha=1 - a)

        def plane_sums():
            for s in range(n_ba):

                def total(s=s):
                    value = mine(s)
                    if s > 0:
                        up(s).wait_recv()
                        value = value + ui[s].astype(F32)
                    if s < n_ba - 1:
                        down(s).wait_recv()
                        value = value + di[s].astype(F32)
                    fin[...] = value

                when(me == s, total)
            for q in range(n_wa):
                pb[q] = fin[q * quarter : (q + 1) * quarter].astype(BF)
            for d in range(1, n_wa):
                to_owner(around(d)).start()

        def spread_sums():
            value = fin[strip(w)]
            for d in range(1, n_wa):
                from_peer(around(d)).wait_recv()
                value = value + pi[around(d)].astype(F32)
            gf[a, strip(w)] = value.astype(BF)
            for d in range(1, n_wa):
                spread(around(d)).start()

        def swap_cores():
            for d in range(1, n_wa):
                gather(around(d)).wait_recv()
            swap().start()

        to_other_core()
        actions = [line(s) for s in range(n_ba - 1)] + [plane_sums, spread_sums, swap_cores]

    def ready_back(g):
        dh[1](g)
        dh[2](g)

    ready_back(0)
    half = rows // 2

    def backward(u):
        g = u // 2

        def head():
            when(g + 1 < groups, lambda: ready_back(g + 1))
            dh[3](g)
            widen(dzp, g, xf)

        when(u % 2 == 0, head)
        conv_back_group(xf, ch, xp, og, ig, gk, g, (u % 2) * half, half)
        for k, act in enumerate(actions):
            when(u == AT[k] * 2 * groups // 12, act)

    loop(2 * groups, backward)

    if not inside:
        gch_out[...] = jnp.sum(gch[...], axis=1)
        gbi_out[...] = jnp.sum(gbi[...], axis=0, keepdims=True)
        gk_out[...] = jnp.sum(gk[...], axis=1)
    else:
        gs[...] = jnp.zeros_like(gs)
        gs[0:49] = jnp.sum(gk[...], axis=1)
        gs[49:54] = jnp.sum(gch[...], axis=1)[:5]
        bias = jnp.sum(gbi[...], axis=0, keepdims=True)
        for b in range(n_ba):
            gs[56 + b : 57 + b] = bias[:, b * C : (b + 1) * C]
        pair = remote(gs, gs_in, t_s, t_r, ha=1 - a)
        pair.start()
        pair.wait_recv()
        gp[w] = (gs[...] + gs_in[...]).astype(BF)
        peer = lambda q: remote(gp.at[w], gp.at[w], tp_s.at[q], tp_r.at[w], wa=q)
        peer_in = lambda q: remote(gp.at[q], gp.at[q], tp_s.at[q], tp_r.at[q], wa=q)
        for d in range(1, n_wa):
            peer(around(d)).start()
        for d in range(1, n_wa):
            peer_in(around(d)).wait_recv()
        tot = gp[0].astype(F32)
        for q in range(1, n_wa):
            tot = tot + gp[q].astype(F32)
        low = tot.astype(BF)
        for b in range(n_ba):
            gz_out[b] = dg(low, place(b, (C, 128), 0), 1, 0).astype(BF)
            line_b = low.astype(F32)[56 + b : 57 + b]
            three = jnp.concatenate([line_b[:, k * 128 : (k + 1) * 128] for k in range(3)], axis=0)
            gz_out[b, 56:64] = jnp.concatenate([three, jnp.zeros((5, 128), F32)], axis=0).astype(BF)
        gz[me] = gz_out[me]
        far = lambda b: remote(gz_out.at[b], gz.at[me], tz_s.at[b], tz_r.at[me], ba=b)
        far_in = lambda b: remote(gz_out.at[b], gz.at[b], tz_s.at[b], tz_r.at[b], ba=b)
        beyond = lambda d: lax.rem(me + d, n_ba)
        for d in range(1, n_ba):
            far(beyond(d)).start()
        swap().wait_recv()
        swap().wait_send()
        for d in range(1, n_ba):
            small_to(d).wait_send()
            w_core(lax.rem(me + d, n_ba)).wait_send()
        for s in range(n_ba):
            to_core(s).wait_send()
            when((s <= me) & (me < n_ba - 1), lambda s=s: w_up_to(s, shard(a, s)).wait_send())
            when((s >= me) & (me > 0), lambda s=s: w_dn_to(s, shard(a, s)).wait_send())
            when(me < s, lambda s=s: up(s).wait_send())
            when(me > s, lambda s=s: down(s).wait_send())
        for d in range(1, n_wa):
            to_owner(around(d)).wait_send()
            spread(around(d)).wait_send()
            peer(around(d)).wait_send()
        pair.wait_send()
        for d in range(1, n_ba):
            far_in(beyond(d)).wait_recv()
        for d in range(1, n_ba):
            far(beyond(d)).wait_send()
        value = gz[0].astype(F32)
        for b in range(1, n_ba):
            value = value + gz[b].astype(F32)
        gsmall[...] = value
    loop(groups, lambda g: (xh[4](g), dh[4](g)))


AT = (1, 3, 5, 7, 8, 10)


def run_main(n_wa, n_ba, x, og, gate, *params):
    groups, rows, cols = x.shape[:3]
    inside = n_ba == 4
    hbm = pl.BlockSpec(memory_space=pl.ANY)
    vm = pl.BlockSpec(memory_space=pltpu.VMEM)
    big = (groups, rows + 2 * R, cols + 2 * R, 8, C)
    dma = pltpu.SemaphoreType.DMA
    S = jax.ShapeDtypeStruct
    V = pltpu.VMEM
    out_shape = [S(x.shape, BF), S(x.shape, BF)]
    scratch = [
        V(big, BF), V(big, BF), V(x.shape, BF), V(big[1:], F32), V((2, rows, cols, 8, C), F32),
        V((8, 8, C), F32), V((8, HID), F32), V((49, 8, C), F32),
        dma((groups, 2)), dma((groups, 2)), dma((groups,)), dma((groups,)),
        dma((groups, 2)), dma((groups, 2)), dma((groups,)), dma((groups,)),
        dma((groups,)), dma((groups,)),
    ]
    if inside:
        out_shape += [S((2, C, C), BF), S((64, 128), F32)]
        quarter = C // n_wa
        sh = (n_ba, C, C)
        scratch += [V((2, C, HID), BF), V((64, C), F32), V((1, HID), F32), V((2, C, HID), F32), V((n_ba, 64, 128), BF)]
        scratch += [dma((n_ba - 1,)), dma((n_ba,)), dma((3,))] + [dma((n_ba,))] * 5
        scratch += [V(sh, BF)] * 6 + [V((C, C), F32), V((n_wa, quarter, C), BF), V((n_wa, quarter, C), BF)]
        scratch += [dma((n_ba,))] * 6 + [dma((n_wa,))] * 4 + [dma, dma]
        scratch += [V((64, C), F32), V((64, C), F32), V((n_wa, 64, C), BF), V((n_ba, 64, 128), BF), V((n_ba, 64, 128), BF)]
        scratch += [dma, dma, dma((n_wa,)), dma((n_wa,)), dma((n_ba,)), dma((n_ba,))]
        in_specs = [hbm, hbm, vm, hbm, hbm]
    else:
        out_shape += [S((2, C, HID), F32), S((8, C), F32), S((1, HID), F32), S((49, C), F32)]
        in_specs = [hbm, hbm] + [vm] * 4
    return pl.pallas_call(
        functools.partial(main_kernel, n_wa, n_ba),
        out_shape=out_shape,
        in_specs=in_specs,
        out_specs=[vm] * len(out_shape),
        scratch_shapes=scratch,
        compiler_params=pltpu.CompilerParams(collective_id=0, has_side_effects=True, vmem_limit_bytes=67043328),
        name="main",
    )(x, og, gate, *params)


def adam_step(master, grad, moment, second, average, rate):
    moment_new = 0.5 * moment + 0.5 * grad
    second_new = 0.5 * second + 0.5 * grad * grad
    correct = 1.0 - 0.5**STEP
    master_new = master - rate * (
        moment_new / correct / (jnp.sqrt(second_new / correct) + 1e-08) + 0.05 * master
    )
    average_new = 0.9 * average + 0.1 * master_new
    return (master_new, moment_new, second_new, average_new)


def local(
    images,
    out_grad,
    keep_mask,
    img_counts,
    mats_master,
    chan_master,
    bias_master,
    mats_moment,
    chan_moment,
    bias_moment,
    mats_second,
    chan_second,
    bias_second,
    mats_average,
    chan_average,
    bias_average,
):
    n_img, rows, cols = images.shape[0], images.shape[1], images.shape[2]
    n_wa, n_ba = lax.axis_size("wa"), lax.axis_size("ba")
    groups = -(-n_img // 8)
    slots = groups * 8
    fill = jnp.arange(n_img, dtype=jnp.int32) < img_counts[0]
    gate = jnp.pad(jnp.where(fill, keep_mask, 0).astype(F32), (0, slots - n_img))
    gate = jnp.broadcast_to(gate.reshape(groups, 8, 1), (groups, 8, C))

    def grouped(v):
        v = jnp.pad(v.transpose(1, 2, 0, 3), ((0, 0), (0, 0), (0, slots - n_img), (0, 0)))
        return v.reshape(rows, cols, groups, 8, C).transpose(2, 0, 1, 3, 4)

    low = lambda v: v.astype(BF)
    if n_ba == 4:
        small = jnp.concatenate(
            [
                jnp.pad(low(chan_master), ((0, 2), (0, 32))),
                jnp.pad(low(bias_master).reshape(3, 128), ((0, 5), (0, 0))),
            ]
        )
        params = (low(mats_master), small)
    else:
        chan_all = lax.all_gather(low(chan_master), "ba", axis=1, tiled=True).astype(F32)
        params = (
            lax.all_gather(low(mats_master), "ba", axis=2, tiled=True),
            jnp.pad(chan_all, ((0, 10), (0, 0))),
            lax.all_gather(low(bias_master), "ba", axis=0, tiled=True).astype(F32)[None],
        )
    out, ig, *grads = run_main(n_wa, n_ba, grouped(images), grouped(out_grad), gate, *params)
    back = lambda v: v.transpose(1, 2, 0, 3, 4).reshape(rows, cols, slots, C)[:, :, :n_img].transpose(2, 0, 1, 3)
    outputs, input_grad = back(out), back(ig)
    if n_ba == 4:
        mats_grad = grads[0].astype(F32)
        chan_grad = grads[1][:54, :96]
        bias_grad = grads[1][56:59].reshape(-1)
    else:
        whole = lax.psum(
            (grads[0], jnp.concatenate([grads[3], grads[1][:5]], axis=0), grads[2][0]), ("ha", "wa")
        )
        mats_grad, chan_grad, bias_grad = (
            lax.psum_scatter(whole[0], "ba", scatter_dimension=2, tiled=True),
            lax.psum_scatter(whole[1], "ba", scatter_dimension=1, tiled=True),
            lax.psum_scatter(whole[2], "ba", scatter_dimension=0, tiled=True),
        )
    mats_new, mats_moment_new, mats_second_new, mats_average_new = adam_step(
        mats_master, mats_grad, mats_moment, mats_second, mats_average, 0.03
    )
    chan_new, chan_moment_new, chan_second_new, chan_average_new = adam_step(
        chan_master, chan_grad, chan_moment, chan_second, chan_average, 0.3
    )
    bias_new, bias_moment_new, bias_second_new, bias_average_new = adam_step(
        bias_master, bias_grad, bias_moment, bias_second, bias_average, 0.3
    )
    return (
        outputs,
        input_grad,
        mats_grad,
        chan_grad,
        bias_grad,
        mats_new,
        chan_new,
        bias_new,
        mats_moment_new,
        chan_moment_new,
        bias_moment_new,
        mats_second_new,
        chan_second_new,
        bias_second_new,
        mats_average_new,
        chan_average_new,
        bias_average_new,
        mats_new.astype(jnp.bfloat16),
        chan_new.astype(jnp.bfloat16),
        bias_new.astype(jnp.bfloat16),
    )


def solution(mesh):
    return jax.shard_map(
        local,
        mesh=mesh,
        in_specs=(
            P("ba", "ha", "wa", None),
            P("ba", "ha", "wa", None),
            P("ba"),
            P("ba"),
            P(None, None, "ba"),
            P(None, "ba"),
            P("ba"),
            P(None, None, "ba"),
            P(None, "ba"),
            P("ba"),
            P(None, None, "ba"),
            P(None, "ba"),
            P("ba"),
            P(None, None, "ba"),
            P(None, "ba"),
            P("ba"),
        ),
        out_specs=(
            P("ba", "ha", "wa", None),
            P("ba", "ha", "wa", None),
            P(None, None, "ba"),
            P(None, "ba"),
            P("ba"),
            P(None, None, "ba"),
            P(None, "ba"),
            P("ba"),
            P(None, None, "ba"),
            P(None, "ba"),
            P("ba"),
            P(None, None, "ba"),
            P(None, "ba"),
            P("ba"),
            P(None, None, "ba"),
            P(None, "ba"),
            P("ba"),
            P(None, None, "ba"),
            P(None, "ba"),
            P("ba"),
        ),
        check_vma=False,
    )
```

```python
import functools

import jax
import jax.numpy as jnp
from jax import lax
from jax.experimental import pallas as pl
from jax.experimental.pallas import tpu as pltpu
from jax.sharding import PartitionSpec as P

C = 384
HID = 1536
KS = 7
R = KS // 2
STEP = 3
F32 = jnp.float32
BF = jnp.bfloat16


MESH = pl.DeviceIdType.MESH


def total(terms):
    while len(terms) > 1:
        terms = [sum(terms[i + 1 : i + 2], terms[i]) for i in range(0, len(terms), 2)]
    return terms[0]


def conv_group(xq, kb, cb, z_ref):
    half, cols = z_ref.shape[0], z_ref.shape[1]

    def step(t, _):
        h = t // 3
        c = pl.ds(pl.multiple_of((t % 3) * 256, 256), 256)
        acc = [jnp.broadcast_to(cb[0:1, c], (8, 256))] * cols
        for i in range(KS):
            row = [xq[h + i, w, :, c] for w in range(cols + KS - 1)]
            tap = [kb[i * KS + j, :, c] for j in range(KS)]
            for w in range(cols):
                acc[w] = acc[w] + total([row[w + j] * tap[j] for j in range(KS)]).astype(F32)
        for w in range(cols):
            z_ref[h, w, :, c] = acc[w]
        return 0

    lax.fori_loop(0, half * 3, step, 0)


def conv_back_group(dq, kb, xm, og, ig, gk, g, first, count):
    half, cols = ig.shape[1] // 2, ig.shape[2]

    def step(t, _):
        h = first + t
        for ct in range(3):
            c = slice(ct * 256, ct * 256 + 256)
            parts = [(h + half * (k // 3), slice(k % 3 * 128, k % 3 * 128 + 128)) for k in (2 * ct, 2 * ct + 1)]
            pair = lambda w: jnp.concatenate([og[g, r, w, :, p].astype(F32) for r, p in parts], axis=1)
            x = [xm[h, w, :, c] for w in range(cols)]
            acc = [pair(w) for w in range(cols)]
            for i in range(KS):
                row = [dq[h + KS - 1 - i, w, :, c] for w in range(cols + KS - 1)]
                tap = [kb[i * KS + j, :, c] for j in range(KS)]
                for w in range(cols):
                    acc[w] = acc[w] + total([row[w + KS - 1 - j] * tap[j] for j in range(KS)]).astype(F32)
                for j in range(KS):
                    part = total([row[w + KS - 1 - j] * x[w] for w in range(cols)])
                    gk[i * KS + j, :, c] = gk[i * KS + j, :, c] + part.astype(F32)
            for w in range(cols):
                for n, (r, p) in enumerate(parts):
                    ig[g, r, w, :, p] = acc[w][:, n * 128 : n * 128 + 128].astype(BF)
        return 0

    lax.fori_loop(0, count, step, 0)


def pack(src, g, dst, row0, col0):
    half = src.shape[1] // 2 - R

    def step(t, _):
        for w in range(dst.shape[1]):
            dst[t, w, :, :C] = src[g, t + row0, w + col0]
            dst[t, w, :, C:] = src[g, t + row0 + half, w + col0]
        return 0

    lax.fori_loop(0, dst.shape[0], step, 0)


def gelu_pair(v):
    e = jnp.exp2(v * v * -0.7213475204444817)
    phi = 0.5 + 0.5 * lax.erf(v * 0.7071067811865476)
    return v * phi, phi + v * e * 0.3989422804014327


def dg(a, b, ca, cb):
    return lax.dot_general(a, b, (((ca,), (cb,)), ((), ())), preferred_element_type=F32)


def mlp_group(z_ref, og, xp, gate_ref, w_all, bi_ref, ch_ref, out, dzp, gw, gch, gbi, g):
    half, cols = z_ref.shape[0], z_ref.shape[1]
    rows = 2 * half
    m = rows * cols * 8
    flat = lambda v: v.reshape(m, C)
    cube = lambda v: v.reshape(rows, cols, 8, C)
    gain, shift, bo, ls = (ch_ref[k : k + 1] for k in range(50, 54))
    z = jnp.concatenate([z_ref[:, :, :, k * C : (k + 1) * C].reshape(m // 2, C) for k in range(2)], axis=0)
    zc = z - jnp.mean(z, axis=1, keepdims=True)
    inv = lax.rsqrt(jnp.mean(zc * zc, axis=1, keepdims=True) + 1e-6)
    xhat = zc * inv
    xn = (xhat * gain + shift).astype(BF)
    gate = gate_ref[g]
    gog = flat(og[g].astype(F32) * gate)
    db = (gog * ls).astype(BF)
    branch = jnp.zeros((m, C), F32)
    dxn = jnp.zeros((m, C), F32)
    for j in range(HID // HC):
        hs = slice(j * HC, (j + 1) * HC)
        pre = dg(xn, w_all[0, :, hs], 1, 0) + bi_ref[0:1, hs]
        da = dg(db, w_all[1, :, hs], 1, 0)
        act, slope = gelu_pair(pre)
        act = act.astype(BF)
        dpre = da * slope
        gbi[:, hs] += jnp.sum(dpre.reshape(m // 8, 8, HC), axis=0)
        dpre = dpre.astype(BF)
        branch += dg(act, w_all[1, :, hs], 1, 1)
        dxn += dg(dpre, w_all[0, :, hs], 1, 1)
        gw[1, :, hs] += dg(db, act, 0, 0)
        gw[0, :, hs] += dg(xn, dpre, 0, 0)
    branch += bo
    mid = (slice(R, R + rows), slice(R, R + cols))
    out[g] = (xp[(g, *mid)].astype(F32) + cube(ls * branch) * gate).astype(BF)
    q = dxn * gain
    m1 = jnp.mean(q, axis=1, keepdims=True)
    m2 = jnp.mean(q * xhat, axis=1, keepdims=True)
    dz = (inv * (q - m1 - xhat * m2)).astype(BF)
    dzp[(g, *mid)] = cube(dz)
    red = lambda v: jnp.sum(v.reshape(m // 8, 8, C), axis=0)
    gch[0] += red(dz.astype(F32))
    gch[1] += red(dxn * xhat)
    gch[2] += red(dxn)
    gch[3] += red(db.astype(F32))
    gch[4] += red(gog * branch)


HC = 512


def exchange(n_wa, rows, cols, pad, cs, cr, rs, rr):
    w = lax.axis_index("wa")
    a = lax.axis_index("ha")
    own = slice(R, R + rows)

    def to_left(g, src=None):
        src = pad.at[g, own, R : 2 * R] if src is None else src
        return pltpu.make_async_remote_copy(
            src, pad.at[g, own, R + cols :], cs.at[g, 0], cr.at[g, 0], device_id={"wa": w - 1}, device_id_type=MESH
        )

    def to_right(g, src=None):
        src = pad.at[g, own, cols : cols + R] if src is None else src
        return pltpu.make_async_remote_copy(
            src, pad.at[g, own, :R], cs.at[g, 1], cr.at[g, 1], device_id={"wa": w + 1}, device_id_type=MESH
        )

    def rows_to(g, up):
        src = pad.at[g, R : 2 * R] if up else pad.at[g, rows : rows + R]
        dst = pad.at[g, R + rows :] if up else pad.at[g, :R]
        return pltpu.make_async_remote_copy(
            src, dst, rs.at[g], rr.at[g], device_id={"ha": 1 - a}, device_id_type=MESH
        )

    def both(g, f0, f1):
        pl.when(a == 0)(lambda: f0(rows_to(g, False)))
        pl.when(a == 1)(lambda: f1(rows_to(g, True)))

    def start_cols(g, left=None, right=None):
        pl.when(w > 0)(lambda: to_left(g, left).start())
        pl.when(w < n_wa - 1)(lambda: to_right(g, right).start())

    def wait_cols(g):
        pl.when(w < n_wa - 1)(lambda: to_left(g).wait_recv())
        pl.when(w > 0)(lambda: to_right(g).wait_recv())

    def start_rows(g):
        both(g, lambda c: c.start(), lambda c: c.start())

    def wait_rows(g):
        rows_to(g, True).wait_recv()

    def drain(g):
        pl.when(w > 0)(lambda: to_left(g).wait_send())
        pl.when(w < n_wa - 1)(lambda: to_right(g).wait_send())
        rows_to(g, True).wait_send()

    def zero_edges(g):
        z = lambda h, v: jnp.zeros((h, v, 8, C), BF)
        pl.when(w == 0)(lambda: pad.__setitem__((g, own, slice(0, R)), z(rows, R)))
        pl.when(w == n_wa - 1)(lambda: pad.__setitem__((g, own, slice(R + cols, 2 * R + cols)), z(rows, R)))
        pl.when(a == 0)(lambda: pad.__setitem__((g, slice(0, R)), z(R, cols + 2 * R)))
        pl.when(a == 1)(lambda: pad.__setitem__((g, slice(R + rows, 2 * R + rows)), z(R, cols + 2 * R)))

    return start_cols, wait_cols, start_rows, wait_rows, drain, zero_edges


def place(b, shape, axis):
    whole = lax.broadcasted_iota(jnp.int32, shape, axis)
    part = lax.broadcasted_iota(jnp.int32, shape, 1 - axis)
    return jnp.where((whole == part + b * 96) & (part < 96), 1.0, 0.0).astype(BF)


def remote(src, dst, send, recv, **where):
    return pltpu.make_async_remote_copy(src, dst, send, recv, device_id=where, device_id_type=MESH)


def main_kernel(n_wa, n_ba, *refs):
    inside = n_ba == 4
    it = iter(refs)
    take = lambda n: [next(it) for _ in range(n)]
    x_hbm, og_hbm, gate_ref = take(3)
    if inside:
        mats_hbm, small_hbm = take(2)
    else:
        w_all, ch, bi = take(3)
    out, ig = take(2)
    if inside:
        gf, gsmall = take(2)
    else:
        gw, gch_out, gbi_out, gk_out = take(4)
    xp, dzp, og, xq, xm, z, gch, gbi, gk, kb, cb = take(11)
    xcs, xcr, xrs, xrr, dcs, dcr, drs, drr, own_sem, og_sem = take(10)
    if inside:
        w_all, ch, bi, gw, s_all = take(5)
        s_send, s_recv, w_own, w_up, w_dn, w_recv, w_cs, w_cr = take(8)
        sb, rb, ub, db, ui, di, fin, pb, pi = take(9)
        r_cs, r_cr, u_s, u_r, d_s, d_r, p_s, p_r, q_s, q_r, f_s, f_r = take(12)
        gs, gs_in, gp, gz, gz_out = take(5)
        t_s, t_r, tp_s, tp_r, tz_s, tz_r = take(6)

    groups, rows, cols = x_hbm.shape[0], x_hbm.shape[1], x_hbm.shape[2]
    w = lax.axis_index("wa")
    a = lax.axis_index("ha")
    me = lax.axis_index("ba")
    mid = (slice(R, R + rows), slice(R, R + cols))
    xh = exchange(n_wa, rows, cols, xp, xcs, xcr, xrs, xrr)
    dh = exchange(n_wa, rows, cols, dzp, dcs, dcr, drs, drr)
    own = lambda g: pltpu.make_async_copy(x_hbm.at[g], xp.at[(g, *mid)], own_sem.at[g])
    ogc = lambda g: pltpu.make_async_copy(og_hbm.at[g], og.at[g], og_sem.at[g])

    def loop(n, f):
        lax.fori_loop(0, n, lambda g, _: (f(g), 0)[1], 0)

    def when(cond, f):
        pl.when(cond)(f)

    barrier = pltpu.get_barrier_semaphore()
    greet = lambda **d: pl.semaphore_signal(barrier, inc=1, device_id=d, device_id_type=MESH)
    for g in range(groups):
        own(g).start()
        ogc(g).start()
    greet(ha=1 - a)
    if inside:
        for d in range(1, n_wa):
            greet(wa=lax.rem(w + d, n_wa))
        for d in range(1, n_ba):
            greet(ba=lax.rem(me + d, n_ba))
        pl.semaphore_wait(barrier, n_wa + n_ba - 1)
    else:
        when(w > 0, lambda: greet(wa=w - 1))
        when(w < n_wa - 1, lambda: greet(wa=w + 1))
        pl.semaphore_wait(barrier, jnp.where(w > 0, 1, 0) + jnp.where(w < n_wa - 1, 1, 0) + 1)

    xh[0](0, x_hbm.at[0, :, 0:R], x_hbm.at[0, :, cols - R : cols])
    if inside:
        lanes = lambda s: pl.ds(pl.multiple_of(s * C, C), C)
        shard = lambda h, s: w_all.at[h, :, lanes(s)]
        small_to = lambda d: remote(
            small_hbm, s_all.at[me], s_send.at[d - 1], s_recv.at[me], ba=lax.rem(me + d, n_ba)
        )
        small_from = lambda s: remote(small_hbm, s_all.at[s], s_send.at[0], s_recv.at[s], ba=me)
        w_mine = lambda h: pltpu.make_async_copy(mats_hbm.at[h], shard(h, me), w_own.at[h])
        s_mine = pltpu.make_async_copy(small_hbm, s_all.at[me], w_own.at[2])
        w_up_to = lambda s, src: remote(src, shard(a, s), w_up.at[s], w_recv.at[s], ba=me + 1)
        w_dn_to = lambda s, src: remote(src, shard(a, s), w_dn.at[s], w_recv.at[s], ba=me - 1)
        w_core = lambda s: remote(shard(a, s), shard(a, s), w_cs.at[s], w_cr.at[s], ha=1 - a)
        for d in range(1, n_ba):
            small_to(d).start()
        when(me < n_ba - 1, lambda: w_up_to(me, mats_hbm.at[a]).start())
        when(me > 0, lambda: w_dn_to(me, mats_hbm.at[a]).start())
        s_mine.start()
        w_mine(0).start()
        w_mine(1).start()

        def hop(d):
            def low():
                w_up_to(me - d, shard(a, me - d)).wait_recv()
                when(me < n_ba - 1, lambda: w_up_to(me - d, shard(a, me - d)).start())
                w_core(me - d).start()

            def high():
                w_dn_to(me + d, shard(a, me + d)).wait_recv()
                when(me > 0, lambda: w_dn_to(me + d, shard(a, me + d)).start())
                w_core(me + d).start()

            when(me >= d, low)
            when(me + d < n_ba, high)

    loop(groups - 1, lambda g: xh[0](g + 1, x_hbm.at[g + 1, :, 0:R], x_hbm.at[g + 1, :, cols - R : cols]))
    loop(groups, lambda g: (xh[5](g), dh[5](g)))
    gw[...] = jnp.zeros_like(gw)
    gch[...] = jnp.zeros_like(gch)
    gbi[...] = jnp.zeros_like(gbi)
    gk[...] = jnp.zeros_like(gk)
    if inside:
        s_mine.wait()
        for d in range(1, n_ba):
            small_from(lax.rem(me + d, n_ba)).wait_recv()
        ch[...] = sum(dg(s_all[b], place(b, (128, C), 1), 1, 0) for b in range(n_ba))
        for b in range(n_ba):
            part = s_all[b, 56:64].astype(F32)
            for k in range(3):
                bi[0:1, b * C + k * 128 : b * C + (k + 1) * 128] = part[k : k + 1]

    for t in range(KS * KS):
        kb[t] = jnp.broadcast_to(jnp.concatenate([ch[t : t + 1]] * 2, axis=1), (8, 2 * C)).astype(BF)
    cb[...] = jnp.concatenate([ch[49:50]] * 2, axis=1)

    def ready(g):
        own(g).wait()
        xh[1](g)
        xh[2](g)

    def conv(g):
        when(g + 1 < groups, lambda: ready(g + 1))
        xh[3](g)
        pack(xp, g, xq, 0, 0)
        conv_group(xq, kb, cb, z.at[g % 2])

    ready(0)
    if inside:
        hop(1)
    conv(0)
    if inside:
        hop(2)
    conv(1)
    if inside:
        hop(3)
        w_mine(0).wait()
        w_mine(1).wait()
        for d in range(1, n_ba):
            w_core(lax.rem(me + d, n_ba)).wait_recv()

    def forward(g):
        ogc(g).wait()
        mlp_group(z.at[g % 2], og, xp, gate_ref, w_all, bi, ch, out, dzp, gw, gch, gbi, g)
        dh[0](g)
        when(g + 2 < groups, lambda: conv(g + 2))

    loop(groups, forward)

    actions = []
    if inside:
        part = lambda s: slice(s * C, (s + 1) * C)
        to_core = lambda s: remote(sb.at[s], rb.at[s], r_cs.at[s], r_cr.at[s], ha=1 - a)
        up = lambda s: remote(ub.at[s], ui.at[s], u_s.at[s], u_r.at[s], ba=me + 1)
        down = lambda s: remote(db.at[s], di.at[s], d_s.at[s], d_r.at[s], ba=me - 1)
        mine = lambda s: gw[a, :, part(s)] + rb[s].astype(F32)

        def to_other_core():
            for s in range(n_ba):
                sb[s] = gw[1 - a, :, part(s)].astype(BF)
            for s in range(n_ba):
                to_core(s).start()

        def line(step):
            def run():
                if step == 0:
                    for s in range(n_ba):
                        to_core(s).wait_recv()

                def go_up():
                    for s in range(n_ba - 1, step, -1):
                        if step:
                            up(s).wait_recv()
                        ub[s] = (mine(s) + ui[s].astype(F32) if step else mine(s)).astype(BF)
                        up(s).start()

                def go_down():
                    for s in range(n_ba - 1 - step):
                        if step:
                            down(s).wait_recv()
                        db[s] = (mine(s) + di[s].astype(F32) if step else mine(s)).astype(BF)
                        down(s).start()

                when(me == step, go_up)
                when(me == n_ba - 1 - step, go_down)

            return run

        quarter = C // n_wa
        strip = lambda q: pl.ds(pl.multiple_of(q * quarter, quarter), quarter)
        around = lambda d: lax.rem(w + d, n_wa)
        to_owner = lambda q: remote(pb.at[q], pi.at[w], p_s.at[q], p_r.at[w], wa=q)
        from_peer = lambda q: remote(pb.at[q], pi.at[q], p_s.at[q], p_r.at[q], wa=q)
        spread = lambda q: remote(gf.at[a, strip(w)], gf.at[a, strip(w)], q_s.at[q], q_r.at[w], wa=q)
        gather = lambda q: remote(gf.at[a, strip(q)], gf.at[a, strip(q)], q_s.at[q], q_r.at[q], wa=q)
        swap = lambda: remote(gf.at[a], gf.at[a], f_s, f_r, ha=1 - a)

        def plane_sums():
            for s in range(n_ba):

                def total(s=s):
                    value = mine(s)
                    if s > 0:
                        up(s).wait_recv()
                        value = value + ui[s].astype(F32)
                    if s < n_ba - 1:
                        down(s).wait_recv()
                        value = value + di[s].astype(F32)
                    fin[...] = value

                when(me == s, total)
            for q in range(n_wa):
                pb[q] = fin[q * quarter : (q + 1) * quarter].astype(BF)
            for d in range(1, n_wa):
                to_owner(around(d)).start()

        def spread_sums():
            value = fin[strip(w)]
            for d in range(1, n_wa):
                from_peer(around(d)).wait_recv()
                value = value + pi[around(d)].astype(F32)
            gf[a, strip(w)] = value.astype(BF)
            for d in range(1, n_wa):
                spread(around(d)).start()

        def swap_cores():
            for d in range(1, n_wa):
                gather(around(d)).wait_recv()
            swap().start()

        to_other_core()
        actions = [line(s) for s in range(n_ba - 1)] + [plane_sums, spread_sums, swap_cores]

    def ready_back(g):
        dh[1](g)
        dh[2](g)

    ready_back(0)
    quart = rows // 4

    def backward(u):
        g = u // 2

        def head():
            when(g + 1 < groups, lambda: ready_back(g + 1))
            dh[3](g)
            pack(dzp, g, xq, 0, 0)
            pack(xp, g, xm, R, R)

        when(u % 2 == 0, head)
        conv_back_group(xq, kb, xm, og, ig, gk, g, (u % 2) * quart, quart)
        for k, act in enumerate(actions):
            when(u == AT[k] * 2 * groups // 12, act)

    loop(2 * groups, backward)

    if not inside:
        gch_out[...] = jnp.sum(gch[...], axis=1)
        gbi_out[...] = jnp.sum(gbi[...], axis=0, keepdims=True)
        both = jnp.sum(gk[...], axis=1)
        gk_out[...] = both[:, :C] + both[:, C:]
    else:
        gs[...] = jnp.zeros_like(gs)
        both = jnp.sum(gk[...], axis=1)
        gs[0:49] = both[:, :C] + both[:, C:]
        gs[49:54] = jnp.sum(gch[...], axis=1)[:5]
        bias = jnp.sum(gbi[...], axis=0, keepdims=True)
        for b in range(n_ba):
            gs[56 + b : 57 + b] = bias[:, b * C : (b + 1) * C]
        pair = remote(gs, gs_in, t_s, t_r, ha=1 - a)
        pair.start()
        pair.wait_recv()
        gp[w] = (gs[...] + gs_in[...]).astype(BF)
        peer = lambda q: remote(gp.at[w], gp.at[w], tp_s.at[q], tp_r.at[w], wa=q)
        peer_in = lambda q: remote(gp.at[q], gp.at[q], tp_s.at[q], tp_r.at[q], wa=q)
        for d in range(1, n_wa):
            peer(around(d)).start()
        for d in range(1, n_wa):
            peer_in(around(d)).wait_recv()
        tot = gp[0].astype(F32)
        for q in range(1, n_wa):
            tot = tot + gp[q].astype(F32)
        low = tot.astype(BF)
        for b in range(n_ba):
            gz_out[b] = dg(low, place(b, (C, 128), 0), 1, 0).astype(BF)
            line_b = low.astype(F32)[56 + b : 57 + b]
            three = jnp.concatenate([line_b[:, k * 128 : (k + 1) * 128] for k in range(3)], axis=0)
            gz_out[b, 56:64] = jnp.concatenate([three, jnp.zeros((5, 128), F32)], axis=0).astype(BF)
        gz[me] = gz_out[me]
        far = lambda b: remote(gz_out.at[b], gz.at[me], tz_s.at[b], tz_r.at[me], ba=b)
        far_in = lambda b: remote(gz_out.at[b], gz.at[b], tz_s.at[b], tz_r.at[b], ba=b)
        beyond = lambda d: lax.rem(me + d, n_ba)
        for d in range(1, n_ba):
            far(beyond(d)).start()
        swap().wait_recv()
        swap().wait_send()
        for d in range(1, n_ba):
            small_to(d).wait_send()
            w_core(lax.rem(me + d, n_ba)).wait_send()
        for s in range(n_ba):
            to_core(s).wait_send()
            when((s <= me) & (me < n_ba - 1), lambda s=s: w_up_to(s, shard(a, s)).wait_send())
            when((s >= me) & (me > 0), lambda s=s: w_dn_to(s, shard(a, s)).wait_send())
            when(me < s, lambda s=s: up(s).wait_send())
            when(me > s, lambda s=s: down(s).wait_send())
        for d in range(1, n_wa):
            to_owner(around(d)).wait_send()
            spread(around(d)).wait_send()
            peer(around(d)).wait_send()
        pair.wait_send()
        for d in range(1, n_ba):
            far_in(beyond(d)).wait_recv()
        for d in range(1, n_ba):
            far(beyond(d)).wait_send()
        value = gz[0].astype(F32)
        for b in range(1, n_ba):
            value = value + gz[b].astype(F32)
        gsmall[...] = value
    loop(groups, lambda g: (xh[4](g), dh[4](g)))


AT = (1, 3, 5, 7, 8, 10)


def run_main(n_wa, n_ba, x, og, gate, *params):
    groups, rows, cols = x.shape[:3]
    inside = n_ba == 4
    hbm = pl.BlockSpec(memory_space=pl.ANY)
    vm = pl.BlockSpec(memory_space=pltpu.VMEM)
    big = (groups, rows + 2 * R, cols + 2 * R, 8, C)
    dma = pltpu.SemaphoreType.DMA
    S = jax.ShapeDtypeStruct
    V = pltpu.VMEM
    out_shape = [S(x.shape, BF), S(x.shape, BF)]
    scratch = [
        V(big, BF), V(big, BF), V(x.shape, BF), V((rows // 2 + 2 * R, cols + 2 * R, 8, 2 * C), BF),
        V((rows // 2, cols, 8, 2 * C), BF), V((2, rows // 2, cols, 8, 2 * C), F32), V((8, 8, C), F32), V((8, HID), F32),
        V((49, 8, 2 * C), F32), V((49, 8, 2 * C), BF), V((1, 2 * C), F32),
        dma((groups, 2)), dma((groups, 2)), dma((groups,)), dma((groups,)),
        dma((groups, 2)), dma((groups, 2)), dma((groups,)), dma((groups,)),
        dma((groups,)), dma((groups,)),
    ]
    if inside:
        out_shape += [S((2, C, C), BF), S((64, 128), F32)]
        quarter = C // n_wa
        sh = (n_ba, C, C)
        scratch += [V((2, C, HID), BF), V((64, C), F32), V((1, HID), F32), V((2, C, HID), F32), V((n_ba, 64, 128), BF)]
        scratch += [dma((n_ba - 1,)), dma((n_ba,)), dma((3,))] + [dma((n_ba,))] * 5
        scratch += [V(sh, BF)] * 6 + [V((C, C), F32), V((n_wa, quarter, C), BF), V((n_wa, quarter, C), BF)]
        scratch += [dma((n_ba,))] * 6 + [dma((n_wa,))] * 4 + [dma, dma]
        scratch += [V((64, C), F32), V((64, C), F32), V((n_wa, 64, C), BF), V((n_ba, 64, 128), BF), V((n_ba, 64, 128), BF)]
        scratch += [dma, dma, dma((n_wa,)), dma((n_wa,)), dma((n_ba,)), dma((n_ba,))]
        in_specs = [hbm, hbm, vm, hbm, hbm]
    else:
        out_shape += [S((2, C, HID), F32), S((8, C), F32), S((1, HID), F32), S((49, C), F32)]
        in_specs = [hbm, hbm] + [vm] * 4
    return pl.pallas_call(
        functools.partial(main_kernel, n_wa, n_ba),
        out_shape=out_shape,
        in_specs=in_specs,
        out_specs=[vm] * len(out_shape),
        scratch_shapes=scratch,
        compiler_params=pltpu.CompilerParams(collective_id=0, has_side_effects=True, vmem_limit_bytes=67043328),
        name="main",
    )(x, og, gate, *params)


def adam_step(master, grad, moment, second, average, rate):
    moment_new = 0.5 * moment + 0.5 * grad
    second_new = 0.5 * second + 0.5 * grad * grad
    correct = 1.0 - 0.5**STEP
    master_new = master - rate * (
        moment_new / correct / (jnp.sqrt(second_new / correct) + 1e-08) + 0.05 * master
    )
    average_new = 0.9 * average + 0.1 * master_new
    return (master_new, moment_new, second_new, average_new)


def local(
    images,
    out_grad,
    keep_mask,
    img_counts,
    mats_master,
    chan_master,
    bias_master,
    mats_moment,
    chan_moment,
    bias_moment,
    mats_second,
    chan_second,
    bias_second,
    mats_average,
    chan_average,
    bias_average,
):
    n_img, rows, cols = images.shape[0], images.shape[1], images.shape[2]
    n_wa, n_ba = lax.axis_size("wa"), lax.axis_size("ba")
    groups = -(-n_img // 8)
    slots = groups * 8
    fill = jnp.arange(n_img, dtype=jnp.int32) < img_counts[0]
    gate = jnp.pad(jnp.where(fill, keep_mask, 0).astype(F32), (0, slots - n_img))
    gate = jnp.broadcast_to(gate.reshape(groups, 8, 1), (groups, 8, C))

    def grouped(v):
        v = jnp.pad(v.transpose(1, 2, 0, 3), ((0, 0), (0, 0), (0, slots - n_img), (0, 0)))
        return v.reshape(rows, cols, groups, 8, C).transpose(2, 0, 1, 3, 4)

    low = lambda v: v.astype(BF)
    if n_ba == 4:
        small = jnp.concatenate(
            [
                jnp.pad(low(chan_master), ((0, 2), (0, 32))),
                jnp.pad(low(bias_master).reshape(3, 128), ((0, 5), (0, 0))),
            ]
        )
        params = (low(mats_master), small)
    else:
        chan_all = lax.all_gather(low(chan_master), "ba", axis=1, tiled=True).astype(F32)
        params = (
            lax.all_gather(low(mats_master), "ba", axis=2, tiled=True),
            jnp.pad(chan_all, ((0, 10), (0, 0))),
            lax.all_gather(low(bias_master), "ba", axis=0, tiled=True).astype(F32)[None],
        )
    out, ig, *grads = run_main(n_wa, n_ba, grouped(images), grouped(out_grad), gate, *params)
    back = lambda v: v.transpose(1, 2, 0, 3, 4).reshape(rows, cols, slots, C)[:, :, :n_img].transpose(2, 0, 1, 3)
    outputs, input_grad = back(out), back(ig)
    if n_ba == 4:
        mats_grad = grads[0].astype(F32)
        chan_grad = grads[1][:54, :96]
        bias_grad = grads[1][56:59].reshape(-1)
    else:
        whole = lax.psum(
            (grads[0], jnp.concatenate([grads[3], grads[1][:5]], axis=0), grads[2][0]), ("ha", "wa")
        )
        mats_grad, chan_grad, bias_grad = (
            lax.psum_scatter(whole[0], "ba", scatter_dimension=2, tiled=True),
            lax.psum_scatter(whole[1], "ba", scatter_dimension=1, tiled=True),
            lax.psum_scatter(whole[2], "ba", scatter_dimension=0, tiled=True),
        )
    mats_new, mats_moment_new, mats_second_new, mats_average_new = adam_step(
        mats_master, mats_grad, mats_moment, mats_second, mats_average, 0.03
    )
    chan_new, chan_moment_new, chan_second_new, chan_average_new = adam_step(
        chan_master, chan_grad, chan_moment, chan_second, chan_average, 0.3
    )
    bias_new, bias_moment_new, bias_second_new, bias_average_new = adam_step(
        bias_master, bias_grad, bias_moment, bias_second, bias_average, 0.3
    )
    return (
        outputs,
        input_grad,
        mats_grad,
        chan_grad,
        bias_grad,
        mats_new,
        chan_new,
        bias_new,
        mats_moment_new,
        chan_moment_new,
        bias_moment_new,
        mats_second_new,
        chan_second_new,
        bias_second_new,
        mats_average_new,
        chan_average_new,
        bias_average_new,
        mats_new.astype(jnp.bfloat16),
        chan_new.astype(jnp.bfloat16),
        bias_new.astype(jnp.bfloat16),
    )


def solution(mesh):
    return jax.shard_map(
        local,
        mesh=mesh,
        in_specs=(
            P("ba", "ha", "wa", None),
            P("ba", "ha", "wa", None),
            P("ba"),
            P("ba"),
            P(None, None, "ba"),
            P(None, "ba"),
            P("ba"),
            P(None, None, "ba"),
            P(None, "ba"),
            P("ba"),
            P(None, None, "ba"),
            P(None, "ba"),
            P("ba"),
            P(None, None, "ba"),
            P(None, "ba"),
            P("ba"),
        ),
        out_specs=(
            P("ba", "ha", "wa", None),
            P("ba", "ha", "wa", None),
            P(None, None, "ba"),
            P(None, "ba"),
            P("ba"),
            P(None, None, "ba"),
            P(None, "ba"),
            P("ba"),
            P(None, None, "ba"),
            P(None, "ba"),
            P("ba"),
            P(None, None, "ba"),
            P(None, "ba"),
            P("ba"),
            P(None, None, "ba"),
            P(None, "ba"),
            P("ba"),
            P(None, None, "ba"),
            P(None, "ba"),
            P("ba"),
        ),
        check_vma=False,
    )
```

```python
import functools

import jax
import jax.numpy as jnp
from jax import lax
from jax.experimental import pallas as pl
from jax.experimental.pallas import tpu as pltpu
from jax.sharding import PartitionSpec as P

C = 384
HID = 1536
KS = 7
R = KS // 2
STEP = 3
F32 = jnp.float32
BF = jnp.bfloat16


MESH = pl.DeviceIdType.MESH


def total(terms):
    while len(terms) > 1:
        terms = [sum(terms[i + 1 : i + 2], terms[i]) for i in range(0, len(terms), 2)]
    return terms[0]


def conv_group(xq, kb, cb, z_ref):
    half, cols = z_ref.shape[0], z_ref.shape[1]

    def step(t, _):
        h = t // 3
        c = pl.ds(pl.multiple_of((t % 3) * 256, 256), 256)
        acc = [jnp.broadcast_to(cb[0:1, c], (8, 256))] * cols
        for i in range(KS):
            row = [xq[h + i, w, :, c] for w in range(cols + KS - 1)]
            tap = [kb[i * KS + j, :, c] for j in range(KS)]
            for w in range(cols):
                acc[w] = acc[w] + total([row[w + j] * tap[j] for j in range(KS)]).astype(F32)
        for w in range(cols):
            z_ref[h, w, :, c] = acc[w]
        return 0

    lax.fori_loop(0, half * 3, step, 0)


def conv_back_group(dq, kb, xm, og, ig, gk, g, first, count):
    half, cols = ig.shape[1] // 2, ig.shape[2]

    def step(t, _):
        h = first + t
        for ct in range(3):
            c = slice(ct * 256, ct * 256 + 256)
            parts = [(h + half * (k // 3), slice(k % 3 * 128, k % 3 * 128 + 128)) for k in (2 * ct, 2 * ct + 1)]
            pair = lambda w: jnp.concatenate([og[g, r, w, :, p].astype(F32) for r, p in parts], axis=1)
            x = [xm[h, w, :, c] for w in range(cols)]
            acc = [pair(w) for w in range(cols)]
            for i in range(KS):
                row = [dq[h + KS - 1 - i, w, :, c] for w in range(cols + KS - 1)]
                tap = [kb[i * KS + j, :, c] for j in range(KS)]
                for w in range(cols):
                    acc[w] = acc[w] + total([row[w + KS - 1 - j] * tap[j] for j in range(KS)]).astype(F32)
                for j in range(KS):
                    part = total([row[w + KS - 1 - j] * x[w] for w in range(cols)])
                    gk[i * KS + j, :, c] = gk[i * KS + j, :, c] + part.astype(F32)
            for w in range(cols):
                for n, (r, p) in enumerate(parts):
                    ig[g, r, w, :, p] = acc[w][:, n * 128 : n * 128 + 128].astype(BF)
        return 0

    lax.fori_loop(0, count, step, 0)


def pack(src, g, dst, row0, col0):
    half = src.shape[1] // 2 - R

    def step(t, _):
        for w in range(dst.shape[1]):
            dst[t, w, :, :C] = src[g, t + row0, w + col0]
            dst[t, w, :, C:] = src[g, t + row0 + half, w + col0]
        return 0

    lax.fori_loop(0, dst.shape[0], step, 0)


def gelu_pair(v):
    e = jnp.exp2(v * v * -0.7213475204444817)
    phi = 0.5 + 0.5 * lax.erf(v * 0.7071067811865476)
    return v * phi, phi + v * e * 0.3989422804014327


def dg(a, b, ca, cb):
    return lax.dot_general(a, b, (((ca,), (cb,)), ((), ())), preferred_element_type=F32)


def mlp_group(z_ref, og, xp, gate_ref, w_all, bi_ref, ch_ref, out, dzp, gw, gch, gbi, g):
    half, cols = z_ref.shape[0], z_ref.shape[1]
    rows = 2 * half
    m = rows * cols * 8
    flat = lambda v: v.reshape(m, C)
    cube = lambda v: v.reshape(rows, cols, 8, C)
    gain, shift, bo, ls = (ch_ref[k : k + 1] for k in range(50, 54))
    z = jnp.concatenate([z_ref[:, :, :, k * C : (k + 1) * C].reshape(m // 2, C) for k in range(2)], axis=0)
    zc = z - jnp.mean(z, axis=1, keepdims=True)
    inv = lax.rsqrt(jnp.mean(zc * zc, axis=1, keepdims=True) + 1e-6)
    xhat = zc * inv
    xn = (xhat * gain + shift).astype(BF)
    gate = gate_ref[g]
    gog = flat(og[g].astype(F32) * gate)
    db = (gog * ls).astype(BF)
    branch = jnp.zeros((m, C), F32)
    dxn = jnp.zeros((m, C), F32)
    for j in range(HID // HC):
        hs = slice(j * HC, (j + 1) * HC)
        pre = dg(xn, w_all[0, :, hs], 1, 0) + bi_ref[0:1, hs]
        da = dg(db, w_all[1, :, hs], 1, 0)
        act, slope = gelu_pair(pre)
        act = act.astype(BF)
        dpre = da * slope
        gbi[:, hs] += jnp.sum(dpre.reshape(m // 8, 8, HC), axis=0)
        dpre = dpre.astype(BF)
        branch += dg(act, w_all[1, :, hs], 1, 1)
        dxn += dg(dpre, w_all[0, :, hs], 1, 1)
        gw[1, :, hs] += dg(db, act, 0, 0)
        gw[0, :, hs] += dg(xn, dpre, 0, 0)
    branch += bo
    mid = (slice(R, R + rows), slice(R, R + cols))
    out[g] = (xp[(g, *mid)].astype(F32) + cube(ls * branch) * gate).astype(BF)
    q = dxn * gain
    m1 = jnp.mean(q, axis=1, keepdims=True)
    m2 = jnp.mean(q * xhat, axis=1, keepdims=True)
    dz = (inv * (q - m1 - xhat * m2)).astype(BF)
    dzp[(g, *mid)] = cube(dz)
    red = lambda v: jnp.sum(v.reshape(m // 8, 8, C), axis=0)
    gch[0] += red(dz.astype(F32))
    gch[1] += red(dxn * xhat)
    gch[2] += red(dxn)
    gch[3] += red(db.astype(F32))
    gch[4] += red(gog * branch)


HC = 512


def exchange(n_wa, rows, cols, pad, cs, cr, rs, rr):
    w = lax.axis_index("wa")
    a = lax.axis_index("ha")
    own = slice(R, R + rows)

    def to_left(g, src=None):
        src = pad.at[g, own, R : 2 * R] if src is None else src
        return pltpu.make_async_remote_copy(
            src, pad.at[g, own, R + cols :], cs.at[g, 0], cr.at[g, 0], device_id={"wa": w - 1}, device_id_type=MESH
        )

    def to_right(g, src=None):
        src = pad.at[g, own, cols : cols + R] if src is None else src
        return pltpu.make_async_remote_copy(
            src, pad.at[g, own, :R], cs.at[g, 1], cr.at[g, 1], device_id={"wa": w + 1}, device_id_type=MESH
        )

    def rows_to(g, up):
        src = pad.at[g, R : 2 * R] if up else pad.at[g, rows : rows + R]
        dst = pad.at[g, R + rows :] if up else pad.at[g, :R]
        return pltpu.make_async_remote_copy(
            src, dst, rs.at[g], rr.at[g], device_id={"ha": 1 - a}, device_id_type=MESH
        )

    def both(g, f0, f1):
        pl.when(a == 0)(lambda: f0(rows_to(g, False)))
        pl.when(a == 1)(lambda: f1(rows_to(g, True)))

    def start_cols(g, left=None, right=None):
        pl.when(w > 0)(lambda: to_left(g, left).start())
        pl.when(w < n_wa - 1)(lambda: to_right(g, right).start())

    def wait_cols(g):
        pl.when(w < n_wa - 1)(lambda: to_left(g).wait_recv())
        pl.when(w > 0)(lambda: to_right(g).wait_recv())

    def start_rows(g):
        both(g, lambda c: c.start(), lambda c: c.start())

    def wait_rows(g):
        rows_to(g, True).wait_recv()

    def drain(g):
        pl.when(w > 0)(lambda: to_left(g).wait_send())
        pl.when(w < n_wa - 1)(lambda: to_right(g).wait_send())
        rows_to(g, True).wait_send()

    def zero_edges(g):
        z = lambda h, v: jnp.zeros((h, v, 8, C), BF)
        pl.when(w == 0)(lambda: pad.__setitem__((g, own, slice(0, R)), z(rows, R)))
        pl.when(w == n_wa - 1)(lambda: pad.__setitem__((g, own, slice(R + cols, 2 * R + cols)), z(rows, R)))
        pl.when(a == 0)(lambda: pad.__setitem__((g, slice(0, R)), z(R, cols + 2 * R)))
        pl.when(a == 1)(lambda: pad.__setitem__((g, slice(R + rows, 2 * R + rows)), z(R, cols + 2 * R)))

    return start_cols, wait_cols, start_rows, wait_rows, drain, zero_edges


def place(b, shape, axis):
    whole = lax.broadcasted_iota(jnp.int32, shape, axis)
    part = lax.broadcasted_iota(jnp.int32, shape, 1 - axis)
    return jnp.where((whole == part + b * 96) & (part < 96), 1.0, 0.0).astype(BF)


def remote(src, dst, send, recv, **where):
    return pltpu.make_async_remote_copy(src, dst, send, recv, device_id=where, device_id_type=MESH)


def main_kernel(n_wa, n_ba, *refs):
    inside = n_ba == 4
    it = iter(refs)
    take = lambda n: [next(it) for _ in range(n)]
    x_hbm, og_hbm, gate_ref = take(3)
    if inside:
        mats_hbm, small_hbm = take(2)
    else:
        w_all, ch, bi = take(3)
    out, ig = take(2)
    if inside:
        gf, gsmall = take(2)
    else:
        gw, gch_out, gbi_out, gk_out = take(4)
    xp, dzp, og, xq, xm, z, gch, gbi, gk, kb, cb = take(11)
    xcs, xcr, xrs, xrr, dcs, dcr, drs, drr, own_sem, og_sem = take(10)
    if inside:
        w_all, ch, bi, gw, s_all = take(5)
        s_send, s_recv, w_own, w_up, w_dn, w_recv, w_cs, w_cr = take(8)
        sb, rb, ub, db, ui, di, fin, pb, pi = take(9)
        r_cs, r_cr, u_s, u_r, d_s, d_r, p_s, p_r, q_s, q_r, f_s, f_r = take(12)
        gs, gs_in, gp, gz, gz_out = take(5)
        t_s, t_r, tp_s, tp_r, tz_s, tz_r = take(6)

    groups, rows, cols = x_hbm.shape[0], x_hbm.shape[1], x_hbm.shape[2]
    w = lax.axis_index("wa")
    a = lax.axis_index("ha")
    me = lax.axis_index("ba")
    mid = (slice(R, R + rows), slice(R, R + cols))
    xh = exchange(n_wa, rows, cols, xp, xcs, xcr, xrs, xrr)
    dh = exchange(n_wa, rows, cols, dzp, dcs, dcr, drs, drr)
    own = lambda g: pltpu.make_async_copy(x_hbm.at[g], xp.at[(g, *mid)], own_sem.at[g])
    ogc = lambda g: pltpu.make_async_copy(og_hbm.at[g], og.at[g], og_sem.at[g])

    def loop(n, f):
        lax.fori_loop(0, n, lambda g, _: (f(g), 0)[1], 0)

    def when(cond, f):
        pl.when(cond)(f)

    barrier = pltpu.get_barrier_semaphore()
    greet = lambda **d: pl.semaphore_signal(barrier, inc=1, device_id=d, device_id_type=MESH)
    for g in range(groups):
        own(g).start()
        ogc(g).start()
    greet(ha=1 - a)
    if inside:
        for d in range(1, n_wa):
            greet(wa=lax.rem(w + d, n_wa))
        for d in range(1, n_ba):
            greet(ba=lax.rem(me + d, n_ba))
        pl.semaphore_wait(barrier, n_wa + n_ba - 1)
    else:
        when(w > 0, lambda: greet(wa=w - 1))
        when(w < n_wa - 1, lambda: greet(wa=w + 1))
        pl.semaphore_wait(barrier, jnp.where(w > 0, 1, 0) + jnp.where(w < n_wa - 1, 1, 0) + 1)

    xh[0](0, x_hbm.at[0, :, 0:R], x_hbm.at[0, :, cols - R : cols])
    if inside:
        lanes = lambda s: pl.ds(pl.multiple_of(s * C, C), C)
        shard = lambda h, s: w_all.at[h, :, lanes(s)]
        small_to = lambda d: remote(
            small_hbm, s_all.at[me], s_send.at[d - 1], s_recv.at[me], ba=lax.rem(me + d, n_ba)
        )
        small_from = lambda s: remote(small_hbm, s_all.at[s], s_send.at[0], s_recv.at[s], ba=me)
        w_mine = lambda h: pltpu.make_async_copy(mats_hbm.at[h], shard(h, me), w_own.at[h])
        s_mine = pltpu.make_async_copy(small_hbm, s_all.at[me], w_own.at[2])
        w_up_to = lambda s, src: remote(src, shard(a, s), w_up.at[s], w_recv.at[s], ba=me + 1)
        w_dn_to = lambda s, src: remote(src, shard(a, s), w_dn.at[s], w_recv.at[s], ba=me - 1)
        w_core = lambda s: remote(shard(a, s), shard(a, s), w_cs.at[s], w_cr.at[s], ha=1 - a)
        for d in range(1, n_ba):
            small_to(d).start()
        when(me < n_ba - 1, lambda: w_up_to(me, mats_hbm.at[a]).start())
        when(me > 0, lambda: w_dn_to(me, mats_hbm.at[a]).start())
        s_mine.start()
        w_mine(0).start()
        w_mine(1).start()

        def hop(d):
            def low():
                w_up_to(me - d, shard(a, me - d)).wait_recv()
                when(me < n_ba - 1, lambda: w_up_to(me - d, shard(a, me - d)).start())
                w_core(me - d).start()

            def high():
                w_dn_to(me + d, shard(a, me + d)).wait_recv()
                when(me > 0, lambda: w_dn_to(me + d, shard(a, me + d)).start())
                w_core(me + d).start()

            when(me >= d, low)
            when(me + d < n_ba, high)

    loop(groups - 1, lambda g: xh[0](g + 1, x_hbm.at[g + 1, :, 0:R], x_hbm.at[g + 1, :, cols - R : cols]))
    loop(groups, lambda g: (xh[5](g), dh[5](g)))
    gw[...] = jnp.zeros_like(gw)
    gch[...] = jnp.zeros_like(gch)
    gbi[...] = jnp.zeros_like(gbi)
    gk[...] = jnp.zeros_like(gk)
    if inside:
        s_mine.wait()
        for d in range(1, n_ba):
            small_from(lax.rem(me + d, n_ba)).wait_recv()
        ch[...] = sum(dg(s_all[b], place(b, (128, C), 1), 1, 0) for b in range(n_ba))
        for b in range(n_ba):
            part = s_all[b, 56:64].astype(F32)
            for k in range(3):
                bi[0:1, b * C + k * 128 : b * C + (k + 1) * 128] = part[k : k + 1]

    for t in range(KS * KS):
        kb[t] = jnp.broadcast_to(jnp.concatenate([ch[t : t + 1]] * 2, axis=1), (8, 2 * C)).astype(BF)
    cb[...] = jnp.concatenate([ch[49:50]] * 2, axis=1)

    def ready(g):
        own(g).wait()
        xh[1](g)
        xh[2](g)

    def conv(g):
        when(g + 1 < groups, lambda: ready(g + 1))
        xh[3](g)
        pack(xp, g, xq, 0, 0)
        conv_group(xq, kb, cb, z.at[g % 2])

    ready(0)
    if inside:
        hop(1)
    conv(0)
    if inside:
        hop(2)
    conv(1)
    if inside:
        hop(3)
        w_mine(0).wait()
        w_mine(1).wait()
        for d in range(1, n_ba):
            w_core(lax.rem(me + d, n_ba)).wait_recv()

    def forward(g):
        ogc(g).wait()
        mlp_group(z.at[g % 2], og, xp, gate_ref, w_all, bi, ch, out, dzp, gw, gch, gbi, g)
        dh[0](g)
        when(g + 2 < groups, lambda: conv(g + 2))

    loop(groups, forward)

    actions = []
    if inside:
        part = lambda s: slice(s * C, (s + 1) * C)
        to_core = lambda s: remote(sb.at[s], rb.at[s], r_cs.at[s], r_cr.at[s], ha=1 - a)
        up = lambda s: remote(ub.at[s], ui.at[s], u_s.at[s], u_r.at[s], ba=me + 1)
        down = lambda s: remote(db.at[s], di.at[s], d_s.at[s], d_r.at[s], ba=me - 1)
        mine = lambda s: gw[a, :, part(s)] + rb[s].astype(F32)

        def to_other_core():
            for s in (3, 0, 2, 1):
                sb[s] = gw[1 - a, :, part(s)].astype(BF)
                to_core(s).start()

        def pass_up(s):
            up(s).wait_recv()
            ub[s] = (mine(s) + ui[s].astype(F32)).astype(BF)
            up(s).start()

        def pass_down(s):
            down(s).wait_recv()
            db[s] = (mine(s) + di[s].astype(F32)).astype(BF)
            down(s).start()

        def from_ends():
            def low():
                for s in range(n_ba - 1, 0, -1):
                    to_core(s).wait_recv()
                    ub[s] = mine(s).astype(BF)
                    up(s).start()
                to_core(0).wait_recv()

            def high():
                for s in range(n_ba - 1):
                    to_core(s).wait_recv()
                    db[s] = mine(s).astype(BF)
                    down(s).start()
                to_core(n_ba - 1).wait_recv()

            def between():
                for s in range(n_ba):
                    to_core(s).wait_recv()

            when(me == 0, low)
            when(me == n_ba - 1, high)
            when((me > 0) & (me < n_ba - 1), between)

        def first_pass():
            when(me == 1, lambda: pass_up(3))
            when(me == 2, lambda: pass_down(0))

        def second_pass():
            def at_1():
                pass_up(2)
                pass_down(0)

            def at_2():
                pass_down(1)
                pass_up(3)

            when(me == 1, at_1)
            when(me == 2, at_2)

        quarter = C // n_wa
        strip = lambda q: pl.ds(pl.multiple_of(q * quarter, quarter), quarter)
        around = lambda d: lax.rem(w + d, n_wa)
        to_owner = lambda q: remote(pb.at[q], pi.at[w], p_s.at[q], p_r.at[w], wa=q)
        from_peer = lambda q: remote(pb.at[q], pi.at[q], p_s.at[q], p_r.at[q], wa=q)
        spread = lambda q: remote(gf.at[a, strip(w)], gf.at[a, strip(w)], q_s.at[q], q_r.at[w], wa=q)
        gather = lambda q: remote(gf.at[a, strip(q)], gf.at[a, strip(q)], q_s.at[q], q_r.at[q], wa=q)
        swap = lambda: remote(gf.at[a], gf.at[a], f_s, f_r, ha=1 - a)

        def plane_sums():
            for s in range(n_ba):

                def total(s=s):
                    value = mine(s)
                    if s > 0:
                        up(s).wait_recv()
                        value = value + ui[s].astype(F32)
                    if s < n_ba - 1:
                        down(s).wait_recv()
                        value = value + di[s].astype(F32)
                    fin[...] = value

                when(me == s, total)
            for q in range(n_wa):
                pb[q] = fin[q * quarter : (q + 1) * quarter].astype(BF)
            for d in range(1, n_wa):
                to_owner(around(d)).start()

        def spread_sums():
            value = fin[strip(w)]
            for d in range(1, n_wa):
                from_peer(around(d)).wait_recv()
                value = value + pi[around(d)].astype(F32)
            gf[a, strip(w)] = value.astype(BF)
            for d in range(1, n_wa):
                spread(around(d)).start()

        def swap_cores():
            for d in range(1, n_wa):
                gather(around(d)).wait_recv()
            swap().start()

        to_other_core()
        actions = [from_ends, first_pass, second_pass, plane_sums]

    def ready_back(g):
        dh[1](g)
        dh[2](g)

    ready_back(0)
    quart = rows // 4

    def backward(u):
        g = u // 2

        def head():
            when(g + 1 < groups, lambda: ready_back(g + 1))
            dh[3](g)
            pack(dzp, g, xq, 0, 0)
            pack(xp, g, xm, R, R)

        when(u % 2 == 0, head)
        conv_back_group(xq, kb, xm, og, ig, gk, g, (u % 2) * quart, quart)
        for k, act in enumerate(actions):
            when(u == AT[k] * 2 * groups // 12, act)

    loop(2 * groups, backward)

    if not inside:
        gch_out[...] = jnp.sum(gch[...], axis=1)
        gbi_out[...] = jnp.sum(gbi[...], axis=0, keepdims=True)
        both = jnp.sum(gk[...], axis=1)
        gk_out[...] = both[:, :C] + both[:, C:]
    else:
        gs[...] = jnp.zeros_like(gs)
        both = jnp.sum(gk[...], axis=1)
        gs[0:49] = both[:, :C] + both[:, C:]
        gs[49:54] = jnp.sum(gch[...], axis=1)[:5]
        bias = jnp.sum(gbi[...], axis=0, keepdims=True)
        for b in range(n_ba):
            gs[56 + b : 57 + b] = bias[:, b * C : (b + 1) * C]
        pair = remote(gs, gs_in, t_s, t_r, ha=1 - a)
        pair.start()
        spread_sums()
        pair.wait_recv()
        gp[w] = (gs[...] + gs_in[...]).astype(BF)
        peer = lambda q: remote(gp.at[w], gp.at[w], tp_s.at[q], tp_r.at[w], wa=q)
        peer_in = lambda q: remote(gp.at[q], gp.at[q], tp_s.at[q], tp_r.at[q], wa=q)
        for d in range(1, n_wa):
            peer(around(d)).start()
        swap_cores()
        for d in range(1, n_wa):
            peer_in(around(d)).wait_recv()
        tot = gp[0].astype(F32)
        for q in range(1, n_wa):
            tot = tot + gp[q].astype(F32)
        low = tot.astype(BF)
        for b in range(n_ba):
            gz_out[b] = dg(low, place(b, (C, 128), 0), 1, 0).astype(BF)
            line_b = low.astype(F32)[56 + b : 57 + b]
            three = jnp.concatenate([line_b[:, k * 128 : (k + 1) * 128] for k in range(3)], axis=0)
            gz_out[b, 56:64] = jnp.concatenate([three, jnp.zeros((5, 128), F32)], axis=0).astype(BF)
        gz[me] = gz_out[me]
        far = lambda b: remote(gz_out.at[b], gz.at[me], tz_s.at[b], tz_r.at[me], ba=b)
        far_in = lambda b: remote(gz_out.at[b], gz.at[b], tz_s.at[b], tz_r.at[b], ba=b)
        beyond = lambda d: lax.rem(me + d, n_ba)
        for d in range(1, n_ba):
            far(beyond(d)).start()
        swap().wait_recv()
        swap().wait_send()
        for d in range(1, n_ba):
            small_to(d).wait_send()
            w_core(lax.rem(me + d, n_ba)).wait_send()
        for s in range(n_ba):
            to_core(s).wait_send()
            when((s <= me) & (me < n_ba - 1), lambda s=s: w_up_to(s, shard(a, s)).wait_send())
            when((s >= me) & (me > 0), lambda s=s: w_dn_to(s, shard(a, s)).wait_send())
            when(me < s, lambda s=s: up(s).wait_send())
            when(me > s, lambda s=s: down(s).wait_send())
        for d in range(1, n_wa):
            to_owner(around(d)).wait_send()
            spread(around(d)).wait_send()
            peer(around(d)).wait_send()
        pair.wait_send()
        for d in range(1, n_ba):
            far_in(beyond(d)).wait_recv()
        for d in range(1, n_ba):
            far(beyond(d)).wait_send()
        value = gz[0].astype(F32)
        for b in range(1, n_ba):
            value = value + gz[b].astype(F32)
        gsmall[...] = value
    loop(groups, lambda g: (xh[4](g), dh[4](g)))


AT = (0, 3, 5, 8)


def run_main(n_wa, n_ba, x, og, gate, *params):
    groups, rows, cols = x.shape[:3]
    inside = n_ba == 4
    hbm = pl.BlockSpec(memory_space=pl.ANY)
    vm = pl.BlockSpec(memory_space=pltpu.VMEM)
    big = (groups, rows + 2 * R, cols + 2 * R, 8, C)
    dma = pltpu.SemaphoreType.DMA
    S = jax.ShapeDtypeStruct
    V = pltpu.VMEM
    out_shape = [S(x.shape, BF), S(x.shape, BF)]
    scratch = [
        V(big, BF), V(big, BF), V(x.shape, BF), V((rows // 2 + 2 * R, cols + 2 * R, 8, 2 * C), BF),
        V((rows // 2, cols, 8, 2 * C), BF), V((2, rows // 2, cols, 8, 2 * C), F32), V((8, 8, C), F32), V((8, HID), F32),
        V((49, 8, 2 * C), F32), V((49, 8, 2 * C), BF), V((1, 2 * C), F32),
        dma((groups, 2)), dma((groups, 2)), dma((groups,)), dma((groups,)),
        dma((groups, 2)), dma((groups, 2)), dma((groups,)), dma((groups,)),
        dma((groups,)), dma((groups,)),
    ]
    if inside:
        out_shape += [S((2, C, C), BF), S((64, 128), F32)]
        quarter = C // n_wa
        sh = (n_ba, C, C)
        scratch += [V((2, C, HID), BF), V((64, C), F32), V((1, HID), F32), V((2, C, HID), F32), V((n_ba, 64, 128), BF)]
        scratch += [dma((n_ba - 1,)), dma((n_ba,)), dma((3,))] + [dma((n_ba,))] * 5
        scratch += [V(sh, BF)] * 6 + [V((C, C), F32), V((n_wa, quarter, C), BF), V((n_wa, quarter, C), BF)]
        scratch += [dma((n_ba,))] * 6 + [dma((n_wa,))] * 4 + [dma, dma]
        scratch += [V((64, C), F32), V((64, C), F32), V((n_wa, 64, C), BF), V((n_ba, 64, 128), BF), V((n_ba, 64, 128), BF)]
        scratch += [dma, dma, dma((n_wa,)), dma((n_wa,)), dma((n_ba,)), dma((n_ba,))]
        in_specs = [hbm, hbm, vm, hbm, hbm]
    else:
        out_shape += [S((2, C, HID), F32), S((8, C), F32), S((1, HID), F32), S((49, C), F32)]
        in_specs = [hbm, hbm] + [vm] * 4
    return pl.pallas_call(
        functools.partial(main_kernel, n_wa, n_ba),
        out_shape=out_shape,
        in_specs=in_specs,
        out_specs=[vm] * len(out_shape),
        scratch_shapes=scratch,
        compiler_params=pltpu.CompilerParams(collective_id=0, has_side_effects=True, vmem_limit_bytes=67043328),
        name="main",
    )(x, og, gate, *params)


def adam_step(master, grad, moment, second, average, rate):
    moment_new = 0.5 * moment + 0.5 * grad
    second_new = 0.5 * second + 0.5 * grad * grad
    correct = 1.0 - 0.5**STEP
    master_new = master - rate * (
        moment_new / correct / (jnp.sqrt(second_new / correct) + 1e-08) + 0.05 * master
    )
    average_new = 0.9 * average + 0.1 * master_new
    return (master_new, moment_new, second_new, average_new)


def local(
    images,
    out_grad,
    keep_mask,
    img_counts,
    mats_master,
    chan_master,
    bias_master,
    mats_moment,
    chan_moment,
    bias_moment,
    mats_second,
    chan_second,
    bias_second,
    mats_average,
    chan_average,
    bias_average,
):
    n_img, rows, cols = images.shape[0], images.shape[1], images.shape[2]
    n_wa, n_ba = lax.axis_size("wa"), lax.axis_size("ba")
    groups = -(-n_img // 8)
    slots = groups * 8
    fill = jnp.arange(n_img, dtype=jnp.int32) < img_counts[0]
    gate = jnp.pad(jnp.where(fill, keep_mask, 0).astype(F32), (0, slots - n_img))
    gate = jnp.broadcast_to(gate.reshape(groups, 8, 1), (groups, 8, C))

    def grouped(v):
        v = jnp.pad(v.transpose(1, 2, 0, 3), ((0, 0), (0, 0), (0, slots - n_img), (0, 0)))
        return v.reshape(rows, cols, groups, 8, C).transpose(2, 0, 1, 3, 4)

    low = lambda v: v.astype(BF)
    if n_ba == 4:
        small = jnp.concatenate(
            [
                jnp.pad(low(chan_master), ((0, 2), (0, 32))),
                jnp.pad(low(bias_master).reshape(3, 128), ((0, 5), (0, 0))),
            ]
        )
        params = (low(mats_master), small)
    else:
        chan_all = lax.all_gather(low(chan_master), "ba", axis=1, tiled=True).astype(F32)
        params = (
            lax.all_gather(low(mats_master), "ba", axis=2, tiled=True),
            jnp.pad(chan_all, ((0, 10), (0, 0))),
            lax.all_gather(low(bias_master), "ba", axis=0, tiled=True).astype(F32)[None],
        )
    out, ig, *grads = run_main(n_wa, n_ba, grouped(images), grouped(out_grad), gate, *params)
    back = lambda v: v.transpose(1, 2, 0, 3, 4).reshape(rows, cols, slots, C)[:, :, :n_img].transpose(2, 0, 1, 3)
    outputs, input_grad = back(out), back(ig)
    if n_ba == 4:
        mats_grad = grads[0].astype(F32)
        chan_grad = grads[1][:54, :96]
        bias_grad = grads[1][56:59].reshape(-1)
    else:
        whole = lax.psum(
            (grads[0], jnp.concatenate([grads[3], grads[1][:5]], axis=0), grads[2][0]), ("ha", "wa")
        )
        mats_grad, chan_grad, bias_grad = (
            lax.psum_scatter(whole[0], "ba", scatter_dimension=2, tiled=True),
            lax.psum_scatter(whole[1], "ba", scatter_dimension=1, tiled=True),
            lax.psum_scatter(whole[2], "ba", scatter_dimension=0, tiled=True),
        )
    mats_new, mats_moment_new, mats_second_new, mats_average_new = adam_step(
        mats_master, mats_grad, mats_moment, mats_second, mats_average, 0.03
    )
    chan_new, chan_moment_new, chan_second_new, chan_average_new = adam_step(
        chan_master, chan_grad, chan_moment, chan_second, chan_average, 0.3
    )
    bias_new, bias_moment_new, bias_second_new, bias_average_new = adam_step(
        bias_master, bias_grad, bias_moment, bias_second, bias_average, 0.3
    )
    return (
        outputs,
        input_grad,
        mats_grad,
        chan_grad,
        bias_grad,
        mats_new,
        chan_new,
        bias_new,
        mats_moment_new,
        chan_moment_new,
        bias_moment_new,
        mats_second_new,
        chan_second_new,
        bias_second_new,
        mats_average_new,
        chan_average_new,
        bias_average_new,
        mats_new.astype(jnp.bfloat16),
        chan_new.astype(jnp.bfloat16),
        bias_new.astype(jnp.bfloat16),
    )


def solution(mesh):
    return jax.shard_map(
        local,
        mesh=mesh,
        in_specs=(
            P("ba", "ha", "wa", None),
            P("ba", "ha", "wa", None),
            P("ba"),
            P("ba"),
            P(None, None, "ba"),
            P(None, "ba"),
            P("ba"),
            P(None, None, "ba"),
            P(None, "ba"),
            P("ba"),
            P(None, None, "ba"),
            P(None, "ba"),
            P("ba"),
            P(None, None, "ba"),
            P(None, "ba"),
            P("ba"),
        ),
        out_specs=(
            P("ba", "ha", "wa", None),
            P("ba", "ha", "wa", None),
            P(None, None, "ba"),
            P(None, "ba"),
            P("ba"),
            P(None, None, "ba"),
            P(None, "ba"),
            P("ba"),
            P(None, None, "ba"),
            P(None, "ba"),
            P("ba"),
            P(None, None, "ba"),
            P(None, "ba"),
            P("ba"),
            P(None, None, "ba"),
            P(None, "ba"),
            P("ba"),
            P(None, None, "ba"),
            P(None, "ba"),
            P("ba"),
        ),
        check_vma=False,
    )
```
